32 devices in a mesh: dp: 4 (over x, core), fsdp: 8 (over z, y).
Axes of the slice: x: 2, y: 2, z: 4, core: 2. Of those that a mesh axis runs over, the one named last changes fastest.
Arguments:
- latents: float32 [64, 256, 384], P(('dp', 'fsdp')), may hold values from -6 to 6
- condition: float32 [64, 384], P(('dp', 'fsdp')), may hold values from -6 to 6
- cotangent: float32 [64, 256, 384], P(('dp', 'fsdp')), may hold values from -6 to 6
- validity: int32 [64], P(('dp', 'fsdp')), may hold values 0 or 1
- params: float32 [2659584], P(('dp', 'fsdp')), as said below
- moment_one: float32 [2659584], P(('dp', 'fsdp'))
- moment_two: float32 [2659584], P(('dp', 'fsdp')), as said below
Outputs:
- block_out: float32 [64, 256, 384], P(('dp', 'fsdp'))
- latents_grad: float32 [64, 256, 384], P(('dp', 'fsdp'))
- condition_grad: float32 [64, 384], P(('dp', 'fsdp'))
- param_grad: float32 [2659584], P(('dp', 'fsdp'))
- new_params: float32 [2659584], P(('dp', 'fsdp'))
- new_moment_one: float32 [2659584], P(('dp', 'fsdp'))
- new_moment_two: float32 [2659584], P(('dp', 'fsdp'))
The draws below stay inside these ranges and needn't reach their ends.
Inputs may be any that keep to these rules, and one draw needn't show every extreme that they name: `params`: each segment of the layout has entries of about the scale of an initialized weight. `moment_two`: positive.
All inputs are finite; a program needn't handle non-finite values. No bound on the sum of `validity` on one device may be relied on, other than what follows from the above.
Results may differ from the reference program's by a relative error of at most 0.02.
The reference program's roundings to bfloat16 on the way count: a program that leaves them out, or rounds other values in their place, can miss the bound.
Values may be sent and summed in bfloat16 or wider, within the bound.
No kernel may reach another device: no remote copies, remote signals or barrier semaphores. Data moves between devices by JAX's collectives and lax.ppermute only.
A program may use at most 128 MiB of HBM per device.

```python
import math
import jax
import jax.numpy as jnp
from jax import lax

D = 384
FF = 1536
HEADS = 6
SEQ = 256
STEP = 3
LATENTS = 64
PARAMS = 2659584


def segment_scale(positions):
    ada_end = D * 6 * D
    qkv_end = ada_end + D * 3 * D
    proj_end = qkv_end + D * D
    first_end = proj_end + D * FF
    second_end = first_end + FF * D
    conditions_list = [positions < ada_end, positions < qkv_end, positions < proj_end, positions < first_end, positions < second_end]
    scales_list = [1.0 / math.sqrt(D), 1.0 / math.sqrt(D), 3.0 / math.sqrt(D), 1.0 / math.sqrt(D), 1.5 / math.sqrt(FF)]
    return jnp.select(conditions_list, scales_list, 0.08)


def draw_params(key, part):
    positions = jnp.arange(PARAMS)
    scales = segment_scale(positions)
    noise = jax.random.normal(key, (PARAMS,), jnp.float32)
    return noise * scales


def draw_moment_one(key, part):
    scale_value = 0.1 / math.sqrt(PARAMS)
    noise = jax.random.normal(key, (PARAMS,), jnp.float32)
    return noise * scale_value


def draw_moment_two(key, part):
    logs = jax.random.uniform(key, (PARAMS,), jnp.float32, math.log(0.2), math.log(2.0))
    return jnp.exp(logs) * (0.001 / PARAMS)


def touch_ends(entries, rng, smallest, largest):
    longest = entries.shape.index(max(entries.shape))
    spots = []
    for shift in (0, 1):
        where = [jax.random.randint(jax.random.fold_in(rng, axis), (), 0, length) for axis, length in enumerate(entries.shape)]
        where[longest] = (where[longest] + shift) % entries.shape[longest]
        spots.append(tuple(where))
    return entries.at[spots[0]].set(smallest).at[spots[1]].set(largest)


def levels(key, shape, cuts, smallest, top_value):
    def one(position, blocks):
        heights = jax.random.uniform(jax.random.fold_in(jax.random.fold_in(key, 6), position), (blocks,), jnp.float32, smallest / len(cuts), top_value / len(cuts))
        return jnp.repeat(jnp.exp(heights), shape[position] // blocks).reshape((-1,) + (1,) * (len(shape) - position - 1))

    gain = one(*cuts[0])
    for cut in cuts[1:]:
        gain = gain * one(*cut)
    return gain


def normal_values(own_key, shape, spread, bound, cuts=(), kind=jnp.bfloat16):
    drawn = spread * jax.random.normal(own_key, shape, jnp.float32)
    if cuts:
        drawn = drawn * levels(own_key, shape, cuts, -0.22, 0.18)
    return jnp.clip(drawn, -bound, bound).astype(kind)


def setup_inputs(seed: int = 0) -> dict:
    key_list = jax.random.split(jax.random.key(seed), 8)
    return {
        "latents": normal_values(key_list[0], (LATENTS, SEQ, D), 1.0, 6.0, ((0, 32),), jnp.float32),
        "condition": normal_values(key_list[1], (LATENTS, D), 1.0, 6.0, ((0, 32),), jnp.float32),
        "cotangent": normal_values(key_list[2], (LATENTS, SEQ, D), 1.0, 6.0, ((0, 32),), jnp.float32),
        "validity": touch_ends((jax.random.randint(key_list[3], (LATENTS,), 0, 4) < 3).astype(jnp.int32), jax.random.fold_in(key_list[3], 1), 0, 1),
        "params": draw_params(jax.random.fold_in(key_list[7], 71), 0),
        "moment_one": draw_moment_one(jax.random.fold_in(key_list[7], 71), 0),
        "moment_two": draw_moment_two(jax.random.fold_in(key_list[7], 71), 0),
    }


NORM_EPS = 1e-06
LEARN_RATE = 0.01
BETA_ONE = 0.9
BETA_TWO = 0.999
ADAM_EPS = 1e-08
WEIGHT_DECAY = 0.1
MAX_NORM = 1.0
GELU_COEF = 0.7978845608028654
CUBIC_COEF = 0.044715

def unpack_params(flat_vector, model_width, hidden_width):
    shape_list = [(model_width, 6 * model_width), (model_width, 3 * model_width), (model_width, model_width), (model_width, hidden_width), (hidden_width, model_width), (6 * model_width,), (model_width,), (model_width,), (model_width,), (hidden_width,), (model_width,)]
    pieces = []
    offset = 0
    for shape_item in shape_list:
        length_item = 1
        for extent in shape_item:
            length_item = length_item * extent
        pieces.append(lax.slice_in_dim(flat_vector, offset, offset + length_item).reshape(shape_item))
        offset = offset + length_item
    matrices = pieces[:5]
    biases = [member.astype(jnp.float32) for member in pieces[5:]]
    return matrices + biases

def gelu_parts(pre_act):
    inner_arg = GELU_COEF * (pre_act + CUBIC_COEF * pre_act * pre_act * pre_act)
    tangent = jnp.tanh(inner_arg)
    gelu_value = 0.5 * pre_act * (1.0 + tangent)
    gelu_slope = 0.5 * (1.0 + tangent) + 0.5 * pre_act * (1.0 - tangent * tangent) * GELU_COEF * (1.0 + 3.0 * CUBIC_COEF * pre_act * pre_act)
    return (gelu_value, gelu_slope)

def normalize(values):
    centered = values - lax.optimization_barrier(jnp.mean(values, axis=-1, keepdims=True))
    inverse_std = lax.rsqrt(lax.optimization_barrier(jnp.mean(centered * centered, axis=-1, keepdims=True)) + NORM_EPS)
    return (centered * inverse_std, inverse_std)

def norm_back(grad_normed, normed, inverse_std):
    first_mean = lax.optimization_barrier(jnp.mean(grad_normed, axis=-1, keepdims=True))
    second_mean = lax.optimization_barrier(jnp.mean(grad_normed * normed, axis=-1, keepdims=True))
    return inverse_std * (grad_normed - first_mean - normed * second_mean)

def forward_one(latent, mod_row, weights):
    weight_ada, weight_qkv, weight_proj, weight_first, weight_second, bias_ada, bias_query, bias_value, bias_proj, bias_first, bias_second = weights
    seq_len = latent.shape[0]
    model_width = latent.shape[1]
    head_width = model_width // HEADS
    scale_factor = head_width ** (-0.5)
    shift_attn, scale_attn, gate_attn, shift_mlp, scale_mlp, gate_mlp = jnp.split(mod_row, 6)
    normed_one, inverse_one = normalize(latent)
    mixed_one = (normed_one * (1.0 + scale_attn) + shift_attn).astype(jnp.bfloat16)
    qkv_bias = jnp.concatenate([bias_query, jnp.zeros_like(bias_query), bias_value])
    qkv_full = jnp.dot(mixed_one, weight_qkv, preferred_element_type=jnp.float32) + qkv_bias
    qkv_half = qkv_full.astype(jnp.bfloat16).reshape(seq_len, 3, HEADS, head_width)
    queries = qkv_half[:, 0].astype(jnp.float32)
    keys_all = qkv_half[:, 1].astype(jnp.float32)
    values_all = qkv_half[:, 2].astype(jnp.float32)
    scores = jnp.einsum('qhd,khd->hqk', queries, keys_all) * scale_factor
    log_norm = jax.nn.logsumexp(scores, axis=-1)
    attn_probs = jnp.exp(scores - log_norm[..., None]).astype(jnp.bfloat16)
    heads_out = jnp.einsum('hqk,khd->qhd', attn_probs.astype(jnp.float32), values_all).reshape(seq_len, model_width)
    heads_half = heads_out.astype(jnp.bfloat16)
    projected = jnp.dot(heads_half, weight_proj, preferred_element_type=jnp.float32) + bias_proj
    middle = latent + gate_attn * projected
    normed_two, inverse_two = normalize(middle)
    mixed_two = (normed_two * (1.0 + scale_mlp) + shift_mlp).astype(jnp.bfloat16)
    pre_act = jnp.dot(mixed_two, weight_first, preferred_element_type=jnp.float32) + bias_first
    gelu_value, gelu_slope = gelu_parts(pre_act)
    gelu_half = gelu_value.astype(jnp.bfloat16)
    mlp_out = jnp.dot(gelu_half, weight_second, preferred_element_type=jnp.float32) + bias_second
    result = middle + gate_mlp * mlp_out
    stored = (normed_one, inverse_one, mixed_one, qkv_half, log_norm, heads_out, heads_half, projected, normed_two, inverse_two, mixed_two, gelu_slope, gelu_half, mlp_out)
    return (result, stored)

def backward_one(upstream, mod_row, stored, weights):
    weight_ada, weight_qkv, weight_proj, weight_first, weight_second, bias_ada, bias_query, bias_value, bias_proj, bias_first, bias_second = weights
    normed_one, inverse_one, mixed_one, qkv_half, log_norm, heads_out, heads_half, projected, normed_two, inverse_two, mixed_two, gelu_slope, gelu_half, mlp_out = stored
    seq_len = upstream.shape[0]
    model_width = upstream.shape[1]
    head_width = model_width // HEADS
    scale_factor = head_width ** (-0.5)
    shift_attn, scale_attn, gate_attn, shift_mlp, scale_mlp, gate_mlp = jnp.split(mod_row, 6)
    grad_gate_mlp = lax.optimization_barrier(jnp.sum(upstream * mlp_out, axis=0))
    grad_mlp = upstream * gate_mlp
    grad_mlp_half = grad_mlp.astype(jnp.bfloat16)
    grad_second = jnp.dot(gelu_half.T, grad_mlp_half, preferred_element_type=jnp.float32)
    grad_bias_second = lax.optimization_barrier(jnp.sum(grad_mlp, axis=0))
    grad_pre = jnp.dot(grad_mlp_half, weight_second.T, preferred_element_type=jnp.float32) * gelu_slope
    grad_pre_half = grad_pre.astype(jnp.bfloat16)
    grad_first = jnp.dot(mixed_two.T, grad_pre_half, preferred_element_type=jnp.float32)
    grad_bias_first = lax.optimization_barrier(jnp.sum(grad_pre, axis=0))
    grad_mixed_two = jnp.dot(grad_pre_half, weight_first.T, preferred_element_type=jnp.float32)
    grad_shift_mlp = lax.optimization_barrier(jnp.sum(grad_mixed_two, axis=0))
    grad_scale_mlp = lax.optimization_barrier(jnp.sum(grad_mixed_two * normed_two, axis=0))
    grad_middle = upstream + norm_back(grad_mixed_two * (1.0 + scale_mlp), normed_two, inverse_two)
    grad_gate_attn = lax.optimization_barrier(jnp.sum(grad_middle * projected, axis=0))
    grad_proj_out = grad_middle * gate_attn
    grad_proj_half = grad_proj_out.astype(jnp.bfloat16)
    grad_proj = jnp.dot(heads_half.T, grad_proj_half, preferred_element_type=jnp.float32)
    grad_bias_proj = lax.optimization_barrier(jnp.sum(grad_proj_out, axis=0))
    grad_heads = jnp.dot(grad_proj_half, weight_proj.T, preferred_element_type=jnp.float32)
    delta_rows = lax.optimization_barrier(jnp.sum((grad_heads * heads_out).reshape(seq_len, HEADS, head_width), axis=-1)).T
    grad_heads_half = grad_heads.astype(jnp.bfloat16).reshape(seq_len, HEADS, head_width).astype(jnp.float32)
    queries = qkv_half[:, 0].astype(jnp.float32)
    keys_all = qkv_half[:, 1].astype(jnp.float32)
    values_all = qkv_half[:, 2].astype(jnp.float32)
    scores = jnp.einsum('qhd,khd->hqk', queries, keys_all) * scale_factor
    probs_full = jnp.exp(scores - log_norm[..., None])
    probs_half = probs_full.astype(jnp.bfloat16).astype(jnp.float32)
    grad_probs = jnp.einsum('qhd,khd->hqk', grad_heads_half, values_all)
    grad_scores = (probs_full * (grad_probs - delta_rows[..., None])).astype(jnp.bfloat16).astype(jnp.float32)
    grad_query = jnp.einsum('hqk,khd->qhd', grad_scores, keys_all) * scale_factor
    grad_key = jnp.einsum('hqk,qhd->khd', grad_scores, queries) * scale_factor
    grad_value = jnp.einsum('hqk,qhd->khd', probs_half, grad_heads_half)
    grad_qkv_half = jnp.stack([grad_query, grad_key, grad_value], axis=1).reshape(seq_len, 3 * model_width).astype(jnp.bfloat16)
    grad_weight_qkv = jnp.dot(mixed_one.T, grad_qkv_half, preferred_element_type=jnp.float32)
    grad_bias_query = lax.optimization_barrier(jnp.sum(grad_query.reshape(seq_len, model_width), axis=0))
    grad_bias_value = lax.optimization_barrier(jnp.sum(grad_value.reshape(seq_len, model_width), axis=0))
    grad_mixed_one = jnp.dot(grad_qkv_half, weight_qkv.T, preferred_element_type=jnp.float32)
    grad_shift_attn = lax.optimization_barrier(jnp.sum(grad_mixed_one, axis=0))
    grad_scale_attn = lax.optimization_barrier(jnp.sum(grad_mixed_one * normed_one, axis=0))
    grad_latent = grad_middle + norm_back(grad_mixed_one * (1.0 + scale_attn), normed_one, inverse_one)
    grad_mod = jnp.concatenate([grad_shift_attn, grad_scale_attn, grad_gate_attn, grad_shift_mlp, grad_scale_mlp, grad_gate_mlp])
    grads = (grad_weight_qkv, grad_proj, grad_first, grad_second, grad_bias_query, grad_bias_value, grad_bias_proj, grad_bias_first, grad_bias_second)
    return (grad_latent, grad_mod, grads)

def reference(latents, condition, cotangent, validity, params, moment_one, moment_two):
    weights = unpack_params(params.astype(jnp.bfloat16), D, FF)
    weight_ada = weights[0]
    bias_ada = weights[5]
    cond_half = jax.nn.silu(condition).astype(jnp.bfloat16)
    modulation = jnp.dot(cond_half, weight_ada, preferred_element_type=jnp.float32) + bias_ada
    upstream_all = cotangent * validity.astype(jnp.float32)[:, None, None]
    zero_grads = tuple([jnp.zeros(member.shape, jnp.float32) for member in weights[1:5] + weights[6:]])

    def latent_step(totals, inputs):
        latent, mod_row, upstream = inputs
        result, stored = forward_one(latent, mod_row, weights)
        grad_latent, grad_mod, grads = backward_one(upstream, mod_row, stored, weights)
        return (jax.tree.map(jnp.add, totals, grads), (result, grad_latent, grad_mod))
    totals, outputs = lax.scan(latent_step, zero_grads, (latents, modulation, upstream_all))
    block_out, latents_grad, grad_modulation = outputs
    grad_mod_half = grad_modulation.astype(jnp.bfloat16)
    grad_weight_ada = jnp.dot(cond_half.T, grad_mod_half, preferred_element_type=jnp.float32)
    grad_bias_ada = lax.optimization_barrier(jnp.sum(grad_modulation, axis=0))
    cond_sig = jax.nn.sigmoid(condition)
    condition_grad = jnp.dot(grad_mod_half, weight_ada.T, preferred_element_type=jnp.float32) * (cond_sig * (1.0 + condition * (1.0 - cond_sig)))
    ordered = [grad_weight_ada, totals[0], totals[1], totals[2], totals[3], grad_bias_ada, totals[4], totals[5], totals[6], totals[7], totals[8]]
    param_grad = jnp.concatenate([member.reshape(-1) for member in ordered])
    square_sum = jnp.sum(param_grad * param_grad)
    clip_factor = jnp.minimum(1.0, MAX_NORM / (jnp.sqrt(square_sum) + NORM_EPS))
    clipped = param_grad * clip_factor
    new_one = BETA_ONE * moment_one + (1.0 - BETA_ONE) * clipped
    new_two = BETA_TWO * moment_two + (1.0 - BETA_TWO) * clipped * clipped
    corrected_one = new_one / (1.0 - BETA_ONE ** STEP)
    corrected_two = new_two / (1.0 - BETA_TWO ** STEP)
    new_params = params - LEARN_RATE * (corrected_one / (jnp.sqrt(corrected_two) + ADAM_EPS) + WEIGHT_DECAY * params)
    return (block_out, latents_grad, condition_grad, param_grad, new_params, new_one, new_two)
```

```python
import functools
import jax
import jax.numpy as jnp
from jax import lax
from jax.experimental import pallas as pl
from jax.experimental.pallas import tpu as pltpu
from jax.sharding import PartitionSpec as P

D = 384
FF = 1536
HEADS = 6
HEAD_DIM = 64
STEP = 3
LANES = 128

NORM_EPS = 1e-06
LEARN_RATE = 0.01
BETA_ONE = 0.9
BETA_TWO = 0.999
ADAM_EPS = 1e-08
WEIGHT_DECAY = 0.1
MAX_NORM = 1.0
GELU_COEF = 0.7978845608028654
CUBIC_COEF = 0.044715


BF = jnp.bfloat16
F32 = jnp.float32

ADA0 = 0
QKV0 = ADA0 + D * 6 * D // LANES
PROJ0 = QKV0 + D * 3 * D // LANES
FIRST0 = PROJ0 + D * D // LANES
SECOND0 = FIRST0 + D * FF // LANES
BIAS0 = SECOND0 + FF * D // LANES
BIAS_LEN = 6 * D + 3 * D + FF + D
TOTAL = BIAS0 * LANES + BIAS_LEN
B_ADA, B_QUERY, B_VALUE, B_PROJ, B_FIRST, B_SECOND = 0, 6 * D, 7 * D, 8 * D, 9 * D, 9 * D + FF

MATRICES = ((ADA0, D, 6 * D), (QKV0, D, 3 * D), (PROJ0, D, D), (FIRST0, D, FF), (SECOND0, FF, D))


def nn(a, b):
    return lax.dot_general(a, b, (((1,), (0,)), ((), ())), preferred_element_type=F32)


def nt(a, b):
    return lax.dot_general(a, b, (((1,), (1,)), ((), ())), preferred_element_type=F32)


def tn(a, b):
    return lax.dot_general(a, b, (((0,), (0,)), ((), ())), preferred_element_type=F32)


def silu(v):
    return v / (1.0 + jnp.exp(-v))


def mean_last(v):
    return jnp.sum(v, axis=-1, keepdims=True) * (1.0 / v.shape[-1])


def shard_geometry(devices):
    length = TOTAL // devices
    starts = [(length * i) // LANES for i in range(devices)]
    shifts = [(length * i) % LANES for i in range(devices)]
    counts = [-(-(shifts[i] + length) // LANES) for i in range(devices)]
    rows = -(-(max(counts) + 1) // 16) * 16
    return length, starts, shifts, counts, rows


def step_kernel(
    devices, seq, batch, slots_in, slots_out,
    me_ref, valid_ref, lat_ref, cond_ref, cot_ref, *rest,
):
    n_in = len(slots_in)
    pieces = rest[:n_in]
    bo_ref, lg_ref, cg_ref = rest[n_in : n_in + 3]
    n_out = len(slots_out)
    outs = rest[n_in + 3 : n_in + 3 + n_out]
    (
        stage, flat, w_ada, w_qkv, w_proj, w_first, w_second, bias,
        normed1, inv1, mixed1, qkv, probs, heads_f, heads_h, projected,
        middle, normed2, inv2, mixed2, slope, gelu_h, mlp_out,
        mod, gmod, gcol, gmlp_h, gpre_h, gmix, gmid, gproj_h, gheads, gqkv_h, cond8, gmod_h,
        sems_in, sems_out,
    ) = rest[n_in + 3 + n_out :]
    length, starts, shifts, counts, rows = shard_geometry(devices)
    me = me_ref[0]
    tokens = batch * seq
    scale = HEAD_DIM ** (-0.5)

    copies = []
    count = 0
    for ref, masks in zip(pieces, slots_in):
        for j, m in enumerate(masks):
            src = ref if len(masks) == 1 else ref.at[j]
            copies.append(
                pltpu.make_async_copy(src, stage.at[jnp.bitwise_xor(me, m)], sems_in.at[count])
            )
            count += 1
    for c in copies:
        c.start()

    chunk = 64
    def norm_one(i, carry):
        rs = pl.ds(pl.multiple_of(i * chunk, chunk), chunk)
        v = lat_ref[rs, :]
        cen = v - mean_last(v)
        inv = lax.rsqrt(mean_last(cen * cen) + NORM_EPS)
        normed1[rs, :] = cen * inv
        inv1[rs, :] = jnp.broadcast_to(inv, (chunk, LANES))
        return carry

    lax.fori_loop(0, tokens // chunk, norm_one, 0)

    for c in copies:
        c.wait()
    for i in range(devices):
        g = starts[i]
        n = counts[i]
        block = stage[i].astype(F32)
        if shifts[i] == 0:
            flat[g : g + n, :] = block[:n]
        else:
            flat[g : g + 1, :] = flat[g : g + 1, :] + block[:1]
            flat[g + 1 : g + n, :] = block[1:n]

    for w, (base, height, width) in zip((w_ada, w_qkv, w_proj, w_first, w_second), MATRICES):
        tiles = width // LANES
        for c in range(tiles):
            w[:, c * LANES : (c + 1) * LANES] = flat[pl.ds(base + c, height, stride=tiles), :].astype(BF)
    for r in range(BIAS_LEN // LANES):
        bias[:, r * LANES : (r + 1) * LANES] = flat[BIAS0 + r : BIAS0 + r + 1, :]

    cond8[...] = jnp.zeros_like(cond8)
    cond8[0:batch, :] = silu(cond_ref[...])
    ch = cond8[...].astype(BF)
    mod[...] = nn(ch, w_ada[...]) + bias[:, B_ADA : B_ADA + 6 * D]

    def part(ref, b, k):
        return ref[pl.ds(b, 1), k * D : (k + 1) * D]

    def mix_one(i, carry):
        b = i // (seq // chunk)
        rs = pl.ds(pl.multiple_of(i * chunk, chunk), chunk)
        mixed1[rs, :] = (normed1[rs, :] * (1.0 + part(mod, b, 1)) + part(mod, b, 0)).astype(BF)
        return carry

    lax.fori_loop(0, tokens // chunk, mix_one, 0)

    for j in range(3):
        cols = slice(j * D, (j + 1) * D)
        acc = nn(mixed1[...], w_qkv[:, cols])
        if j == 0:
            acc = acc + bias[:, B_QUERY : B_QUERY + D]
        if j == 2:
            acc = acc + bias[:, B_VALUE : B_VALUE + D]
        qkv[:, cols] = acc.astype(BF)

    lane = lax.broadcasted_iota(jnp.int32, (1, LANES), 1)
    low = lane < HEAD_DIM
    zero_bf = jnp.zeros((), BF)

    def keep(v, half):
        return jnp.where(low if half == 0 else jnp.logical_not(low), v, zero_bf)

    pairs = HEADS // 2

    def attn(b, carry):
        rs = pl.ds(pl.multiple_of(b * seq, seq), seq)
        for h in range(pairs):
            q = qkv[rs, h * LANES : (h + 1) * LANES]
            k = qkv[rs, D + h * LANES : D + (h + 1) * LANES]
            v = qkv[rs, 2 * D + h * LANES : 2 * D + (h + 1) * LANES]
            res = []
            for half in range(2):
                s = nt(keep(q, half), k) * scale
                e = jnp.exp(s - jnp.max(s, axis=-1, keepdims=True))
                p = e * (1.0 / jnp.sum(e, axis=-1, keepdims=True))
                probs[b * HEADS + 2 * h + half] = p
                res.append(nn(p.astype(BF), v))
            o = jnp.where(low, res[0], res[1])
            heads_f[rs, h * LANES : (h + 1) * LANES] = o
            heads_h[rs, h * LANES : (h + 1) * LANES] = o.astype(BF)
        return carry

    lax.fori_loop(0, batch, attn, 0)

    projected[...] = nn(heads_h[...], w_proj[...]) + bias[:, B_PROJ : B_PROJ + D]

    def mid(i, carry):
        b = i // (seq // chunk)
        rs = pl.ds(pl.multiple_of(i * chunk, chunk), chunk)
        m = lat_ref[rs, :] + part(mod, b, 2) * projected[rs, :]
        middle[rs, :] = m
        cen = m - mean_last(m)
        inv = lax.rsqrt(mean_last(cen * cen) + NORM_EPS)
        n2 = cen * inv
        normed2[rs, :] = n2
        inv2[rs, :] = jnp.broadcast_to(inv, (chunk, LANES))
        mixed2[rs, :] = (n2 * (1.0 + part(mod, b, 4)) + part(mod, b, 3)).astype(BF)
        return carry

    lax.fori_loop(0, tokens // chunk, mid, 0)

    fchunk = 256
    for j in range(FF // fchunk):
        cols = slice(j * fchunk, (j + 1) * fchunk)
        u = nn(mixed2[...], w_first[:, cols]) + bias[:, B_FIRST + j * fchunk : B_FIRST + (j + 1) * fchunk]
        uu = u * u
        t = jnp.tanh(GELU_COEF * (u + CUBIC_COEF * uu * u))
        half_u = 0.5 * u
        gelu_h[:, cols] = (half_u * (1.0 + t)).astype(BF)
        slope[:, cols] = 0.5 * (1.0 + t) + half_u * (1.0 - t * t) * GELU_COEF * (
            1.0 + 3.0 * CUBIC_COEF * uu
        )
    mlp_out[...] = nn(gelu_h[...], w_second[...]) + bias[:, B_SECOND : B_SECOND + D]

    gcol[...] = jnp.zeros_like(gcol)
    gmod[...] = jnp.zeros_like(gmod)

    def add_col(ref, b, k, v):
        ref[pl.ds(b, 1), k * D : (k + 1) * D] += jnp.sum(v, axis=0, keepdims=True)

    def out_step(i, carry):
        b = i // (seq // chunk)
        rs = pl.ds(pl.multiple_of(i * chunk, chunk), chunk)
        mo = mlp_out[rs, :]
        gate = part(mod, b, 5)
        bo_ref[rs, :] = middle[rs, :] + gate * mo
        up = cot_ref[rs, :] * valid_ref[b].astype(F32)
        add_col(gmod, b, 5, up * mo)
        gm = up * gate
        gcol[:, B_SECOND : B_SECOND + D] += jnp.sum(gm, axis=0, keepdims=True)
        gmlp_h[rs, :] = gm.astype(BF)
        return carry

    lax.fori_loop(0, tokens // chunk, out_step, 0)

    def put(base, tiles, height, row0, c0, value):
        for c in range(value.shape[1] // LANES):
            flat[pl.ds(base + row0 * tiles + c0 + c, height, stride=tiles), :] = value[
                :, c * LANES : (c + 1) * LANES
            ]

    for j in range(FF // D):
        rr = slice(j * D, (j + 1) * D)
        put(SECOND0, D // LANES, D, j * D, 0, tn(gelu_h[:, rr], gmlp_h[...]))
    for j in range(FF // fchunk):
        cols = slice(j * fchunk, (j + 1) * fchunk)
        gp = nt(gmlp_h[...], w_second[cols, :]) * slope[:, cols]
        gcol[:, B_FIRST + j * fchunk : B_FIRST + (j + 1) * fchunk] = jnp.sum(gp, axis=0, keepdims=True)
        gpre_h[:, cols] = gp.astype(BF)
    for j in range(FF // D):
        cols = slice(j * D, (j + 1) * D)
        put(FIRST0, FF // LANES, D, 0, j * (D // LANES), tn(mixed2[...], gpre_h[:, cols]))
    gmix[...] = nt(gpre_h[...], w_first[...])

    def back_two(i, carry):
        b = i // (seq // chunk)
        rs = pl.ds(pl.multiple_of(i * chunk, chunk), chunk)
        g = gmix[rs, :]
        n2 = normed2[rs, :]
        add_col(gmod, b, 3, g)
        add_col(gmod, b, 4, g * n2)
        e = g * (1.0 + part(mod, b, 4))
        up = cot_ref[rs, :] * valid_ref[b].astype(F32)
        inv = inv2[rs, 0:1]
        gm = up + inv * (e - mean_last(e) - n2 * mean_last(e * n2))
        gmid[rs, :] = gm
        add_col(gmod, b, 2, gm * projected[rs, :])
        gp = gm * part(mod, b, 2)
        gcol[:, B_PROJ : B_PROJ + D] += jnp.sum(gp, axis=0, keepdims=True)
        gproj_h[rs, :] = gp.astype(BF)
        return carry

    lax.fori_loop(0, tokens // chunk, back_two, 0)

    put(PROJ0, D // LANES, D, 0, 0, tn(heads_h[...], gproj_h[...]))
    gheads[...] = nt(gproj_h[...], w_proj[...])

    def attn_back(b, carry):
        rs = pl.ds(pl.multiple_of(b * seq, seq), seq)
        for h in range(pairs):
            ls = slice(h * LANES, (h + 1) * LANES)
            q = qkv[rs, h * LANES : (h + 1) * LANES]
            k = qkv[rs, D + h * LANES : D + (h + 1) * LANES]
            v = qkv[rs, 2 * D + h * LANES : 2 * D + (h + 1) * LANES]
            gh = gheads[rs, ls]
            prod = gh * heads_f[rs, ls]
            ghh = gh.astype(BF)
            dq, dk, dv = [], [], []
            for half in range(2):
                delta = jnp.sum(
                    jnp.where(low if half == 0 else jnp.logical_not(low), prod, 0.0),
                    axis=-1, keepdims=True,
                )
                p = probs[b * HEADS + 2 * h + half]
                gp = nt(keep(ghh, half), v)
                gs = (p * (gp - delta)).astype(BF)
                dq.append(nn(gs, k))
                dk.append(tn(gs, q))
                dv.append(tn(p.astype(BF), ghh))
            gq = jnp.where(low, dq[0], dq[1]) * scale
            gk = jnp.where(low, dk[0], dk[1]) * scale
            gv = jnp.where(low, dv[0], dv[1])
            gcol[:, B_QUERY + h * LANES : B_QUERY + (h + 1) * LANES] += jnp.sum(gq, axis=0, keepdims=True)
            gcol[:, B_VALUE + h * LANES : B_VALUE + (h + 1) * LANES] += jnp.sum(gv, axis=0, keepdims=True)
            gqkv_h[rs, h * LANES : (h + 1) * LANES] = gq.astype(BF)
            gqkv_h[rs, D + h * LANES : D + (h + 1) * LANES] = gk.astype(BF)
            gqkv_h[rs, 2 * D + h * LANES : 2 * D + (h + 1) * LANES] = gv.astype(BF)
        return carry

    lax.fori_loop(0, batch, attn_back, 0)

    for j in range(3):
        cols = slice(j * D, (j + 1) * D)
        put(QKV0, 3 * D // LANES, D, 0, j * (D // LANES), tn(mixed1[...], gqkv_h[:, cols]))
    gmix[...] = nt(gqkv_h[...], w_qkv[...])

    def back_one(i, carry):
        b = i // (seq // chunk)
        rs = pl.ds(pl.multiple_of(i * chunk, chunk), chunk)
        g = gmix[rs, :]
        n1 = normed1[rs, :]
        add_col(gmod, b, 0, g)
        add_col(gmod, b, 1, g * n1)
        e = g * (1.0 + part(mod, b, 1))
        inv = inv1[rs, 0:1]
        lg_ref[rs, :] = gmid[rs, :] + inv * (e - mean_last(e) - n1 * mean_last(e * n1))
        return carry

    lax.fori_loop(0, tokens // chunk, back_one, 0)

    gmod_h[...] = gmod[...].astype(BF)
    for j in range(6):
        cols = slice(j * D, (j + 1) * D)
        put(ADA0, 6 * D // LANES, D, 0, j * (D // LANES), tn(ch, gmod_h[:, cols]))
    gcol[:, B_ADA : B_ADA + 6 * D] = jnp.sum(gmod[...], axis=0, keepdims=True)
    cg = nt(gmod_h[...], w_ada[...])[0:batch]
    cv = cond_ref[...]
    sig = 1.0 / (1.0 + jnp.exp(-cv))
    cg_ref[...] = cg * (sig * (1.0 + cv * (1.0 - sig)))

    for r in range(BIAS_LEN // LANES):
        flat[BIAS0 + r : BIAS0 + r + 1, :] = gcol[:, r * LANES : (r + 1) * LANES]

    for i in range(devices):
        g = starts[i]
        stage[i] = flat[g : g + rows, :].astype(BF)
    copies = []
    count = 0
    for ref, masks in zip(outs, slots_out):
        for j, m in enumerate(masks):
            dst = ref if len(masks) == 1 else ref.at[j]
            copies.append(
                pltpu.make_async_copy(stage.at[jnp.bitwise_xor(me, m)], dst, sems_out.at[count])
            )
            count += 1
    for c in copies:
        c.start()
    for c in copies:
        c.wait()


def run_step(devices, me, validity, latents, condition, cotangent, pieces, slots_in, slots_out):
    batch, seq, _ = latents.shape
    tokens = batch * seq
    length, starts, shifts, counts, rows = shard_geometry(devices)
    flat_rows = -(-(starts[-1] + rows) // 16) * 16
    vm = pl.BlockSpec(memory_space=pltpu.VMEM)
    sm = pl.BlockSpec(memory_space=pltpu.SMEM)
    hb = pl.BlockSpec(memory_space=pl.ANY)
    out_shape = [
        jax.ShapeDtypeStruct((tokens, D), F32),
        jax.ShapeDtypeStruct((tokens, D), F32),
        jax.ShapeDtypeStruct((batch, D), F32),
    ] + [
        jax.ShapeDtypeStruct((rows, LANES) if len(m) == 1 else (len(m), rows, LANES), BF)
        for m in slots_out
    ]
    V = pltpu.VMEM
    scratch = [
        V((devices, rows, LANES), BF),
        V((flat_rows, LANES), F32),
        V((D, 6 * D), BF), V((D, 3 * D), BF), V((D, D), BF), V((D, FF), BF), V((FF, D), BF),
        V((1, BIAS_LEN), F32),
        V((tokens, D), F32), V((tokens, LANES), F32), V((tokens, D), BF), V((tokens, 3 * D), BF),
        V((batch * HEADS, seq, seq), F32), V((tokens, D), F32), V((tokens, D), BF), V((tokens, D), F32),
        V((tokens, D), F32), V((tokens, D), F32), V((tokens, LANES), F32), V((tokens, D), BF),
        V((tokens, FF), F32), V((tokens, FF), BF), V((tokens, D), F32),
        V((8, 6 * D), F32), V((8, 6 * D), F32), V((1, BIAS_LEN), F32),
        V((tokens, D), BF), V((tokens, FF), BF), V((tokens, D), F32), V((tokens, D), F32),
        V((tokens, D), BF), V((tokens, D), F32), V((tokens, 3 * D), BF), V((8, D), F32), V((8, 6 * D), BF),
        pltpu.SemaphoreType.DMA((devices,)), pltpu.SemaphoreType.DMA((devices,)),
    ]
    body = functools.partial(step_kernel, devices, seq, batch, slots_in, slots_out)
    res = pl.pallas_call(
        body,
        out_shape=out_shape,
        in_specs=[sm, sm, vm, vm, vm] + [hb] * len(pieces),
        out_specs=[vm, vm, vm] + [hb] * len(slots_out),
        scratch_shapes=scratch,
        compiler_params=pltpu.CompilerParams(vmem_limit_bytes=60 * 1024 * 1024),
        name="step",
    )(
        me, validity, latents.reshape(tokens, D), condition, cotangent.reshape(tokens, D), *pieces
    )
    return res[0], res[1], res[2], res[3:]


def shift_kernel(s_ref, x_ref, o_ref):
    s = s_ref[0]
    rolled = pltpu.roll(x_ref[...], s, 1)
    above = pltpu.roll(rolled, 1, 0)
    lane = lax.broadcasted_iota(jnp.int32, rolled.shape, 1)
    o_ref[...] = jnp.where(lane < s, above, rolled).astype(BF)


def shift_shard(shift, params, rows):
    padded = jnp.pad(params, (0, rows * LANES - params.shape[0])).reshape(rows, LANES)
    return pl.pallas_call(
        shift_kernel,
        out_shape=jax.ShapeDtypeStruct((rows, LANES), BF),
        in_specs=[pl.BlockSpec(memory_space=pltpu.SMEM), pl.BlockSpec(memory_space=pltpu.VMEM)],
        out_specs=pl.BlockSpec(memory_space=pltpu.VMEM),
        name="shift",
    )(shift, padded)


def unshift_kernel(length, n, s_ref, *refs):
    s = s_ref[0]
    total = refs[0][...].astype(F32)
    for r in refs[1:n]:
        total = total + r[...].astype(F32)
    g_ref, sq_ref = refs[n:]
    rows = total.shape[0]
    back = jnp.where(s == 0, 0, LANES - s)
    rolled = pltpu.roll(total, back, 1)
    below = pltpu.roll(rolled, rows - 1, 0)
    lane = lax.broadcasted_iota(jnp.int32, rolled.shape, 1)
    row = lax.broadcasted_iota(jnp.int32, rolled.shape, 0)
    out = jnp.where(lane < LANES - s, rolled, below)
    out = jnp.where(row * LANES + lane < length, out, 0.0)
    g_ref[...] = out
    sq_ref[...] = jnp.full(sq_ref.shape, jnp.sum(out * out), F32)


def unshift(shift, parts, length):
    rows = parts[0].shape[0]
    return pl.pallas_call(
        functools.partial(unshift_kernel, length, len(parts)),
        out_shape=[jax.ShapeDtypeStruct((rows, LANES), F32), jax.ShapeDtypeStruct((8, LANES), F32)],
        in_specs=[pl.BlockSpec(memory_space=pltpu.SMEM)]
        + [pl.BlockSpec(memory_space=pltpu.VMEM)] * len(parts),
        out_specs=[pl.BlockSpec(memory_space=pltpu.VMEM)] * 2,
        name="unshift",
    )(shift, *parts)


TREE = (
    ((1, 0, 0), "x", 1, (0, 0, 0)),
    ((0, 1, 0), "y", 1, (0, 0, 0)),
    ((0, 0, 1), "z", 1, (0, 0, 0)),
    ((0, 0, 2), "z", 2, (0, 0, 0)),
    ((0, 0, 3), "z", 3, (0, 0, 0)),
    ((1, 1, 0), "x", 1, (0, 1, 0)),
    ((1, 0, 1), "z", 1, (1, 0, 0)),
    ((0, 1, 1), "z", 1, (0, 1, 0)),
    ((1, 0, 2), "x", 1, (0, 0, 2)),
    ((0, 1, 2), "y", 1, (0, 0, 2)),
    ((1, 0, 3), "x", 1, (0, 0, 3)),
    ((0, 1, 3), "y", 1, (0, 0, 3)),
    ((1, 1, 1), "y", 1, (1, 0, 1)),
    ((1, 1, 2), "x", 1, (0, 1, 2)),
    ((1, 1, 3), "y", 1, (1, 0, 3)),
)
OFFSETS = ((0, 0, 0),) + tuple(t[0] for t in TREE)


def hop(v, kind, d):
    if kind == "x":
        return lax.ppermute(v, "dp", [(i, i ^ 2) for i in range(4)])
    if kind == "core":
        return lax.ppermute(v, "dp", [(i, i ^ 1) for i in range(4)])
    if kind == "y":
        return lax.ppermute(v, "fsdp", [(i, i ^ 1) for i in range(8)])
    return lax.ppermute(v, "fsdp", [(i, i ^ (2 * d)) for i in range(8)])


def mask_of(offset, core):
    return offset[0] * 16 + core * 8 + offset[2] * 2 + offset[1]


def local(latents, condition, cotangent, validity, params, moment_one, moment_two):
    outer = lax.axis_size("dp")
    inner = lax.axis_size("fsdp")
    devices = outer * inner
    both = ("dp", "fsdp")
    me = lax.axis_index("dp") * inner + lax.axis_index("fsdp")
    length, starts, shifts, counts, rows = shard_geometry(devices)
    shift = ((me * (length % LANES)) % LANES).astype(jnp.int32).reshape(1)
    own = shift_shard(shift, params, rows)
    if (outer, inner) == (4, 8):
        got = {(0, 0, 0): own}
        for off, kind, d, src in TREE:
            got[off] = hop(got[src], kind, d)
        pieces = [got[o] for o in OFFSETS]
        pieces = pieces + [hop(v, "core", 1) for v in pieces]
        slots_in = [(mask_of(o, c),) for c in (0, 1) for o in OFFSETS]
        slots_out = [tuple(mask_of(o, c) for o in OFFSETS) for c in (0, 1)]
        bo, lg, cg, (mine, other) = run_step(
            devices, me.astype(jnp.int32).reshape(1), validity, latents, condition, cotangent,
            pieces, slots_in, slots_out,
        )
        theirs = hop(other, "core", 1)
        sums = {
            o: (mine[j].astype(F32) + theirs[j].astype(F32)) for j, o in enumerate(OFFSETS)
        }
        pending = {o: [] for o in OFFSETS}
        for off, kind, d, src in reversed(TREE):
            total = sums[off]
            for extra in pending[off]:
                total = total + extra.astype(F32)
            pending[src].append(hop(total.astype(BF), kind, d))
        parts = [sums[0, 0, 0].astype(BF)] + pending[0, 0, 0]
    else:
        gathered = lax.all_gather(own, both, axis=0, tiled=False)
        every = [tuple(range(devices))]
        bo, lg, cg, (chunks,) = run_step(
            devices, jnp.zeros((1,), jnp.int32), validity, latents, condition, cotangent,
            [gathered], every, every,
        )
        parts = [lax.psum_scatter(chunks, both, scatter_dimension=0, tiled=False)]
    grad, squares = unshift(shift, parts, length)
    for axis, size in (("dp", outer), ("fsdp", inner)):
        d = 1
        while d < size:
            squares = squares + lax.ppermute(squares, axis, [(i, i ^ d) for i in range(size)])
            d *= 2
    clip_factor = jnp.minimum(1.0, MAX_NORM / (jnp.sqrt(squares[0, 0]) + NORM_EPS))
    grad_shard = grad.reshape(-1)[:length]
    clipped = grad_shard * clip_factor
    new_one = BETA_ONE * moment_one + (1.0 - BETA_ONE) * clipped
    new_two = BETA_TWO * moment_two + (1.0 - BETA_TWO) * clipped * clipped
    corrected_one = new_one / (1.0 - BETA_ONE**STEP)
    corrected_two = new_two / (1.0 - BETA_TWO**STEP)
    new_params = params - LEARN_RATE * (
        corrected_one / (jnp.sqrt(corrected_two) + ADAM_EPS) + WEIGHT_DECAY * params
    )
    return (
        bo.reshape(latents.shape), lg.reshape(latents.shape), cg,
        grad_shard, new_params, new_one, new_two,
    )


def solution(mesh):
    both = ("dp", "fsdp")
    in_specs = (
        P(both, None, None), P(both, None), P(both, None, None),
        P(both), P(both), P(both), P(both),
    )
    out_specs = (
        P(both, None, None), P(both, None, None), P(both, None),
        P(both), P(both), P(both), P(both),
    )
    return jax.shard_map(local, mesh=mesh, in_specs=in_specs, out_specs=out_specs, check_vma=False)
```

```python
import functools
import jax
import jax.numpy as jnp
from jax import lax
from jax.experimental import pallas as pl
from jax.experimental.pallas import tpu as pltpu
from jax.sharding import PartitionSpec as P


D = 384
FF = 1536
HEADS = 6
HEAD_DIM = 64
STEP = 3
LANES = 128

NORM_EPS = 1e-06
LEARN_RATE = 0.01
BETA_ONE = 0.9
BETA_TWO = 0.999
ADAM_EPS = 1e-08
WEIGHT_DECAY = 0.1
MAX_NORM = 1.0
GELU_COEF = 0.7978845608028654
CUBIC_COEF = 0.044715

VMEM_LIMIT = 52 * 1024 * 1024


BF = jnp.bfloat16
F32 = jnp.float32

ADA0 = 0
QKV0 = ADA0 + D * 6 * D // LANES
PROJ0 = QKV0 + D * 3 * D // LANES
FIRST0 = PROJ0 + D * D // LANES
SECOND0 = FIRST0 + D * FF // LANES
BIAS0 = SECOND0 + FF * D // LANES
BIAS_LEN = 6 * D + 3 * D + FF + D
TOTAL = BIAS0 * LANES + BIAS_LEN
B_ADA, B_QUERY, B_VALUE, B_PROJ, B_FIRST, B_SECOND = 0, 6 * D, 7 * D, 8 * D, 9 * D, 9 * D + FF

MATRICES = ((ADA0, D, 6 * D), (QKV0, D, 3 * D), (PROJ0, D, D), (FIRST0, D, FF), (SECOND0, FF, D))


def nn(a, b):
    return lax.dot_general(a, b, (((1,), (0,)), ((), ())), preferred_element_type=F32)


def nt(a, b):
    return lax.dot_general(a, b, (((1,), (1,)), ((), ())), preferred_element_type=F32)


def tn(a, b):
    return lax.dot_general(a, b, (((0,), (0,)), ((), ())), preferred_element_type=F32)


def silu(v):
    return v / (1.0 + jnp.exp(-v))


def mean_last(v):
    return jnp.sum(v, axis=-1, keepdims=True) * (1.0 / v.shape[-1])


def shard_geometry(devices):
    length = TOTAL // devices
    starts = [(length * i) // LANES for i in range(devices)]
    shifts = [(length * i) % LANES for i in range(devices)]
    counts = [-(-(shifts[i] + length) // LANES) for i in range(devices)]
    rows = -(-(max(counts) + 1) // 16) * 16
    return length, starts, shifts, counts, rows


def step_kernel(
    devices, seq, batch, slots_in, slots_out,
    me_ref, valid_ref, lat_hbm, cond_ref, cot_hbm, *rest,
):
    n_in = len(slots_in)
    pieces = rest[:n_in]
    bo_hbm, lg_hbm, cg_ref = rest[n_in : n_in + 3]
    n_out = len(slots_out)
    outs = rest[n_in + 3 : n_in + 3 + n_out]
    (
        stage, flat, w_ada, w_qkv, w_proj, w_first, w_second, bias,
        normed1, inv1, mixed1, qkv, probs, heads_f, heads_h, projected,
        middle, normed2, inv2, mixed2, slope, gelu_h, mlp_out,
        mod, gmod, gcol, gmlp_h, gpre_h, gmix, cond8, gmod_h,
        lat_ref, cot_ref, bo_ref, lg_ref, sem_lat, sem_cot, sem_bo, sem_lg, sems_in, sems_out,
    ) = rest[n_in + 3 + n_out :]
    gmid, gheads, gproj_h, gqkv_h = middle, mlp_out, gmlp_h, gpre_h
    _, starts, shifts, counts, rows = shard_geometry(devices)
    tokens = batch * seq
    scale = HEAD_DIM ** (-0.5)
    me = me_ref[0]
    core_one = me_ref[1] == 1

    def owner(masks):
        return jnp.bitwise_xor(me, jnp.where(core_one, masks[1], masks[0]))

    copy_lat = pltpu.make_async_copy(lat_hbm, lat_ref, sem_lat)
    copy_cot = pltpu.make_async_copy(cot_hbm, cot_ref, sem_cot)
    copy_bo = pltpu.make_async_copy(bo_ref, bo_hbm, sem_bo)
    copy_lg = pltpu.make_async_copy(lg_ref, lg_hbm, sem_lg)
    copy_lat.start()
    copies = []
    for ref, slots in zip(pieces, slots_in):
        for j, masks in enumerate(slots):
            src = ref if len(slots) == 1 else ref.at[j]
            copies.append(
                pltpu.make_async_copy(src, stage.at[owner(masks)], sems_in.at[len(copies)])
            )
            copies[-1].start()
    copy_cot.start()

    chunk = 256

    def norm_one(i, carry):
        rs = pl.ds(pl.multiple_of(i * chunk, chunk), chunk)
        v = lat_ref[rs, :]
        cen = v - mean_last(v)
        inv = lax.rsqrt(mean_last(cen * cen) + NORM_EPS)
        normed1[rs, :] = cen * inv
        inv1[rs, :] = jnp.broadcast_to(inv, (chunk, LANES))
        return carry

    copy_lat.wait()
    lax.fori_loop(0, tokens // chunk, norm_one, 0)

    for c in copies:
        c.wait()
    for i in range(devices):
        g = starts[i]
        n = counts[i]
        block = stage[i].astype(F32)
        if shifts[i] == 0:
            flat[g : g + n, :] = block[:n]
        else:
            flat[g : g + 1, :] = flat[g : g + 1, :] + block[:1]
            flat[g + 1 : g + n, :] = block[1:n]

    for w, (base, height, width) in zip((w_ada, w_qkv, w_proj, w_first, w_second), MATRICES):
        tiles = width // LANES
        for c in range(tiles):
            w[:, c * LANES : (c + 1) * LANES] = flat[pl.ds(base + c, height, stride=tiles), :].astype(BF)
    for r in range(BIAS_LEN // LANES):
        bias[:, r * LANES : (r + 1) * LANES] = flat[BIAS0 + r : BIAS0 + r + 1, :]

    cond8[...] = jnp.zeros_like(cond8)
    cond8[0:batch, :] = silu(cond_ref[...])
    ch = cond8[...].astype(BF)
    mod[...] = nn(ch, w_ada[...]) + bias[:, B_ADA : B_ADA + 6 * D]

    def part(ref, b, k):
        return ref[pl.ds(b, 1), k * D : (k + 1) * D]

    def mix_one(i, carry):
        b = i // (seq // chunk)
        rs = pl.ds(pl.multiple_of(i * chunk, chunk), chunk)
        mixed1[rs, :] = (normed1[rs, :] * (1.0 + part(mod, b, 1)) + part(mod, b, 0)).astype(BF)
        return carry

    lax.fori_loop(0, tokens // chunk, mix_one, 0)

    for j in range(3):
        cols = slice(j * D, (j + 1) * D)
        acc = nn(mixed1[...], w_qkv[:, cols])
        if j == 0:
            acc = acc + bias[:, B_QUERY : B_QUERY + D]
        if j == 2:
            acc = acc + bias[:, B_VALUE : B_VALUE + D]
        qkv[:, cols] = acc.astype(BF)

    lane = lax.broadcasted_iota(jnp.int32, (1, LANES), 1)
    low = lane < HEAD_DIM
    zero_bf = jnp.zeros((), BF)

    def keep(v, half):
        return jnp.where(low if half == 0 else jnp.logical_not(low), v, zero_bf)

    pairs = HEADS // 2

    def attn(b, carry):
        rs = pl.ds(pl.multiple_of(b * seq, seq), seq)
        for h in range(pairs):
            q = qkv[rs, h * LANES : (h + 1) * LANES]
            k = qkv[rs, D + h * LANES : D + (h + 1) * LANES]
            v = qkv[rs, 2 * D + h * LANES : 2 * D + (h + 1) * LANES]
            res = []
            for half in range(2):
                s = nt(keep(q, half), k) * scale
                e = jnp.exp(s - jnp.max(s, axis=-1, keepdims=True))
                p = e * (1.0 / jnp.sum(e, axis=-1, keepdims=True))
                probs[b * HEADS + 2 * h + half] = p
                res.append(nn(p.astype(BF), v))
            o = jnp.where(low, res[0], res[1])
            heads_f[rs, h * LANES : (h + 1) * LANES] = o
            heads_h[rs, h * LANES : (h + 1) * LANES] = o.astype(BF)
        return carry

    lax.fori_loop(0, batch, attn, 0)

    projected[...] = nn(heads_h[...], w_proj[...]) + bias[:, B_PROJ : B_PROJ + D]

    def mid(i, carry):
        b = i // (seq // chunk)
        rs = pl.ds(pl.multiple_of(i * chunk, chunk), chunk)
        m = lat_ref[rs, :] + part(mod, b, 2) * projected[rs, :]
        middle[rs, :] = m
        cen = m - mean_last(m)
        inv = lax.rsqrt(mean_last(cen * cen) + NORM_EPS)
        n2 = cen * inv
        normed2[rs, :] = n2
        inv2[rs, :] = jnp.broadcast_to(inv, (chunk, LANES))
        mixed2[rs, :] = (n2 * (1.0 + part(mod, b, 4)) + part(mod, b, 3)).astype(BF)
        return carry

    lax.fori_loop(0, tokens // chunk, mid, 0)

    fchunk = 256
    for j in range(FF // fchunk):
        cols = slice(j * fchunk, (j + 1) * fchunk)
        u = nn(mixed2[...], w_first[:, cols]) + bias[:, B_FIRST + j * fchunk : B_FIRST + (j + 1) * fchunk]
        uu = u * u
        t = jnp.tanh(GELU_COEF * (u + CUBIC_COEF * uu * u))
        half_u = 0.5 * u
        gelu_h[:, cols] = (half_u * (1.0 + t)).astype(BF)
        slope[:, cols] = 0.5 * (1.0 + t) + half_u * (1.0 - t * t) * GELU_COEF * (
            1.0 + 3.0 * CUBIC_COEF * uu
        )
    mlp_out[...] = nn(gelu_h[...], w_second[...]) + bias[:, B_SECOND : B_SECOND + D]

    gcol[...] = jnp.zeros_like(gcol)
    gmod[...] = jnp.zeros_like(gmod)

    def add_col(ref, b, k, v):
        ref[pl.ds(b, 1), k * D : (k + 1) * D] += jnp.sum(v, axis=0, keepdims=True)

    def out_step(i, carry):
        b = i // (seq // chunk)
        rs = pl.ds(pl.multiple_of(i * chunk, chunk), chunk)
        mo = mlp_out[rs, :]
        gate = part(mod, b, 5)
        bo_ref[rs, :] = middle[rs, :] + gate * mo
        up = cot_ref[rs, :] * valid_ref[b].astype(F32)
        add_col(gmod, b, 5, up * mo)
        gm = up * gate
        gcol[:, B_SECOND : B_SECOND + D] += jnp.sum(gm, axis=0, keepdims=True)
        gmlp_h[rs, :] = gm.astype(BF)
        return carry

    copy_cot.wait()
    lax.fori_loop(0, tokens // chunk, out_step, 0)
    copy_bo.start()

    def put(base, tiles, height, row0, c0, value):
        for c in range(value.shape[1] // LANES):
            flat[pl.ds(base + row0 * tiles + c0 + c, height, stride=tiles), :] = value[
                :, c * LANES : (c + 1) * LANES
            ]

    for j in range(FF // D):
        rr = slice(j * D, (j + 1) * D)
        put(SECOND0, D // LANES, D, j * D, 0, tn(gelu_h[:, rr], gmlp_h[...]))
    for j in range(FF // fchunk):
        cols = slice(j * fchunk, (j + 1) * fchunk)
        gp = nt(gmlp_h[...], w_second[cols, :]) * slope[:, cols]
        gcol[:, B_FIRST + j * fchunk : B_FIRST + (j + 1) * fchunk] = jnp.sum(gp, axis=0, keepdims=True)
        gpre_h[:, cols] = gp.astype(BF)
    for j in range(FF // D):
        cols = slice(j * D, (j + 1) * D)
        put(FIRST0, FF // LANES, D, 0, j * (D // LANES), tn(mixed2[...], gpre_h[:, cols]))
    gmix[...] = nt(gpre_h[...], w_first[...])

    def back_two(i, carry):
        b = i // (seq // chunk)
        rs = pl.ds(pl.multiple_of(i * chunk, chunk), chunk)
        g = gmix[rs, :]
        n2 = normed2[rs, :]
        add_col(gmod, b, 3, g)
        add_col(gmod, b, 4, g * n2)
        e = g * (1.0 + part(mod, b, 4))
        up = cot_ref[rs, :] * valid_ref[b].astype(F32)
        inv = inv2[rs, 0:1]
        gm = up + inv * (e - mean_last(e) - n2 * mean_last(e * n2))
        gmid[rs, :] = gm
        add_col(gmod, b, 2, gm * projected[rs, :])
        gp = gm * part(mod, b, 2)
        gcol[:, B_PROJ : B_PROJ + D] += jnp.sum(gp, axis=0, keepdims=True)
        gproj_h[rs, :] = gp.astype(BF)
        return carry

    lax.fori_loop(0, tokens // chunk, back_two, 0)

    put(PROJ0, D // LANES, D, 0, 0, tn(heads_h[...], gproj_h[...]))
    gheads[...] = nt(gproj_h[...], w_proj[...])

    def attn_back(b, carry):
        rs = pl.ds(pl.multiple_of(b * seq, seq), seq)
        for h in range(pairs):
            ls = slice(h * LANES, (h + 1) * LANES)
            q = qkv[rs, h * LANES : (h + 1) * LANES]
            k = qkv[rs, D + h * LANES : D + (h + 1) * LANES]
            v = qkv[rs, 2 * D + h * LANES : 2 * D + (h + 1) * LANES]
            gh = gheads[rs, ls]
            prod = gh * heads_f[rs, ls]
            ghh = gh.astype(BF)
            dq, dk, dv = [], [], []
            for half in range(2):
                delta = jnp.sum(
                    jnp.where(low if half == 0 else jnp.logical_not(low), prod, 0.0),
                    axis=-1, keepdims=True,
                )
                p = probs[b * HEADS + 2 * h + half]
                gp = nt(keep(ghh, half), v)
                gs = (p * (gp - delta)).astype(BF)
                dq.append(nn(gs, k))
                dk.append(tn(gs, q))
                dv.append(tn(p.astype(BF), ghh))
            gq = jnp.where(low, dq[0], dq[1]) * scale
            gk = jnp.where(low, dk[0], dk[1]) * scale
            gv = jnp.where(low, dv[0], dv[1])
            gcol[:, B_QUERY + h * LANES : B_QUERY + (h + 1) * LANES] += jnp.sum(gq, axis=0, keepdims=True)
            gcol[:, B_VALUE + h * LANES : B_VALUE + (h + 1) * LANES] += jnp.sum(gv, axis=0, keepdims=True)
            gqkv_h[rs, h * LANES : (h + 1) * LANES] = gq.astype(BF)
            gqkv_h[rs, D + h * LANES : D + (h + 1) * LANES] = gk.astype(BF)
            gqkv_h[rs, 2 * D + h * LANES : 2 * D + (h + 1) * LANES] = gv.astype(BF)
        return carry

    lax.fori_loop(0, batch, attn_back, 0)

    for j in range(3):
        cols = slice(j * D, (j + 1) * D)
        put(QKV0, 3 * D // LANES, D, 0, j * (D // LANES), tn(mixed1[...], gqkv_h[:, cols]))
    gmix[...] = nt(gqkv_h[:, : 3 * D], w_qkv[...])

    def back_one(i, carry):
        b = i // (seq // chunk)
        rs = pl.ds(pl.multiple_of(i * chunk, chunk), chunk)
        g = gmix[rs, :]
        n1 = normed1[rs, :]
        add_col(gmod, b, 0, g)
        add_col(gmod, b, 1, g * n1)
        e = g * (1.0 + part(mod, b, 1))
        inv = inv1[rs, 0:1]
        lg_ref[rs, :] = gmid[rs, :] + inv * (e - mean_last(e) - n1 * mean_last(e * n1))
        return carry

    lax.fori_loop(0, tokens // chunk, back_one, 0)
    copy_lg.start()

    gmod_h[...] = gmod[...].astype(BF)
    for j in range(6):
        cols = slice(j * D, (j + 1) * D)
        put(ADA0, 6 * D // LANES, D, 0, j * (D // LANES), tn(ch, gmod_h[:, cols]))
    gcol[:, B_ADA : B_ADA + 6 * D] = jnp.sum(gmod[...], axis=0, keepdims=True)
    cg = nt(gmod_h[...], w_ada[...])[0:batch]
    cv = cond_ref[...]
    sig = 1.0 / (1.0 + jnp.exp(-cv))
    cg_ref[...] = cg * (sig * (1.0 + cv * (1.0 - sig)))

    for r in range(BIAS_LEN // LANES):
        flat[BIAS0 + r : BIAS0 + r + 1, :] = gcol[:, r * LANES : (r + 1) * LANES]

    for i in range(devices):
        g = starts[i]
        stage[i] = flat[g : g + rows, :].astype(BF)
    copies = [copy_bo, copy_lg]
    for ref, slots in zip(outs, slots_out):
        for j, masks in enumerate(slots):
            copies.append(
                pltpu.make_async_copy(stage.at[owner(masks)], ref.at[j], sems_out.at[len(copies) - 2])
            )
            copies[-1].start()
    for c in copies:
        c.wait()


def run_step(
    devices, place, validity, latents, condition, cotangent, pieces, slots_in, slots_out
):
    batch, seq, _ = latents.shape
    tokens = batch * seq
    _, starts, _, _, rows = shard_geometry(devices)
    flat_rows = -(-(starts[-1] + rows) // 16) * 16
    vm = pl.BlockSpec(memory_space=pltpu.VMEM)
    hb = pl.BlockSpec(memory_space=pl.ANY)
    sm = pl.BlockSpec(memory_space=pltpu.SMEM)
    out_shape = [
        jax.ShapeDtypeStruct((tokens, D), F32),
        jax.ShapeDtypeStruct((tokens, D), F32),
        jax.ShapeDtypeStruct((batch, D), F32),
    ] + [
        jax.ShapeDtypeStruct((len(slots), rows, LANES), BF) for slots in slots_out
    ]
    V = pltpu.VMEM
    scratch = [
        V((devices, rows, LANES), BF),
        V((flat_rows, LANES), F32),
        V((D, 6 * D), BF), V((D, 3 * D), BF), V((D, D), BF), V((D, FF), BF), V((FF, D), BF),
        V((1, BIAS_LEN), F32),
        V((tokens, D), F32), V((tokens, LANES), F32), V((tokens, D), BF), V((tokens, 3 * D), BF),
        V((batch * HEADS, seq, seq), F32), V((tokens, D), F32), V((tokens, D), BF), V((tokens, D), F32),
        V((tokens, D), F32), V((tokens, D), F32), V((tokens, LANES), F32), V((tokens, D), BF),
        V((tokens, FF), F32), V((tokens, FF), BF), V((tokens, D), F32),
        V((8, 6 * D), F32), V((8, 6 * D), F32), V((1, BIAS_LEN), F32),
        V((tokens, D), BF), V((tokens, FF), BF), V((tokens, D), F32), V((8, D), F32), V((8, 6 * D), BF),
        V((tokens, D), F32), V((tokens, D), F32), V((tokens, D), F32), V((tokens, D), F32),
        pltpu.SemaphoreType.DMA, pltpu.SemaphoreType.DMA, pltpu.SemaphoreType.DMA, pltpu.SemaphoreType.DMA,
        pltpu.SemaphoreType.DMA((devices,)), pltpu.SemaphoreType.DMA((devices,)),
    ]
    body = functools.partial(step_kernel, devices, seq, batch, slots_in, slots_out)
    res = pl.pallas_call(
        body,
        out_shape=out_shape,
        in_specs=[sm, sm, hb, vm, hb] + [hb] * len(pieces),
        out_specs=[hb, hb, vm] + [hb] * len(slots_out),
        scratch_shapes=scratch,
        compiler_params=pltpu.CompilerParams(vmem_limit_bytes=VMEM_LIMIT),
        name="step",
    )(
        place, validity, latents.reshape(tokens, D), condition, cotangent.reshape(tokens, D), *pieces
    )
    return res[0], res[1], res[2], res[3:]


def shift_kernel(s_ref, x_ref, o_ref):
    s = s_ref[0]
    rolled = pltpu.roll(x_ref[...], s, 1)
    above = pltpu.roll(rolled, 1, 0)
    lane = lax.broadcasted_iota(jnp.int32, rolled.shape, 1)
    o_ref[...] = jnp.where(lane < s, above, rolled).astype(BF)


def shift_shard(shift, params, rows):
    padded = jnp.pad(params, (0, rows * LANES - params.shape[0])).reshape(rows, LANES)
    return pl.pallas_call(
        shift_kernel,
        out_shape=jax.ShapeDtypeStruct((rows, LANES), BF),
        in_specs=[pl.BlockSpec(memory_space=pltpu.SMEM), pl.BlockSpec(memory_space=pltpu.VMEM)],
        out_specs=pl.BlockSpec(memory_space=pltpu.VMEM),
        name="shift",
    )(shift, padded)


def unshift_kernel(length, n, s_ref, *refs):
    s = s_ref[0]
    total = refs[0][...].astype(F32)
    for r in refs[1:n]:
        total = total + r[...].astype(F32)
    g_ref, sq_ref = refs[n:]
    rows = total.shape[0]
    back = jnp.where(s == 0, 0, LANES - s)
    rolled = pltpu.roll(total, back, 1)
    below = pltpu.roll(rolled, rows - 1, 0)
    lane = lax.broadcasted_iota(jnp.int32, rolled.shape, 1)
    row = lax.broadcasted_iota(jnp.int32, rolled.shape, 0)
    out = jnp.where(lane < LANES - s, rolled, below)
    out = jnp.where(row * LANES + lane < length, out, 0.0)
    g_ref[...] = out
    sq_ref[...] = jnp.full(sq_ref.shape, jnp.sum(out * out), F32)


def unshift(shift, parts, length):
    rows = parts[0].shape[0]
    return pl.pallas_call(
        functools.partial(unshift_kernel, length, len(parts)),
        out_shape=[jax.ShapeDtypeStruct((rows, LANES), F32), jax.ShapeDtypeStruct((8, LANES), F32)],
        in_specs=[pl.BlockSpec(memory_space=pltpu.SMEM)]
        + [pl.BlockSpec(memory_space=pltpu.VMEM)] * len(parts),
        out_specs=[pl.BlockSpec(memory_space=pltpu.VMEM)] * 2,
        name="unshift",
    )(shift, *parts)


HOPS = {"a": 16, "b": 1, "z1": 2, "z2": 4, "z3": 6}
GATHER = (
    (16, "a"), (4, "z2"), (1, "b"), (2, "z1"), (18, "z1"), (22, "z3"), (17, "a"), (7, "z3"),
    (5, "b"), (20, "a"), (19, "z1"), (3, "b"), (21, "a"), (6, "z1"), (23, "b"),
)
SCATTER = (
    (23, "z3"), (20, "a"), (7, "z1"), (21, "a"), (3, "b"), (19, "z1"), (6, "z1"), (22, "z3"),
    (5, "b"), (18, "a"), (17, "b"), (4, "z2"), (2, "z1"), (1, "b"), (16, "a"),
)
GATHER_NODES = (0,) + tuple(n for n, _ in GATHER)
SCATTER_NODES = tuple(n for n, _ in SCATTER) + (0,)
GROUP = 4


def swap(node):
    return (node & 6) | (16 if node & 1 else 0) | (1 if node & 16 else 0)


def hop(v, kind):
    pairs = []
    for i in range(32):
        m = 8 if kind == "core" else HOPS[kind]
        pairs.append((i, i ^ (swap(m) if i & 8 and kind != "core" else m)))
    return lax.ppermute(v, ("dp", "fsdp"), pairs)


def near(nodes):
    return [(n, swap(n)) for n in nodes]


def far(nodes):
    return [(8 ^ swap(n), 8 ^ n) for n in nodes]


def local(latents, condition, cotangent, validity, params, moment_one, moment_two):
    outer = lax.axis_size("dp")
    inner = lax.axis_size("fsdp")
    devices = outer * inner
    both = ("dp", "fsdp")
    me = (lax.axis_index("dp") * inner + lax.axis_index("fsdp")).astype(jnp.int32)
    length, _, _, _, rows = shard_geometry(devices)
    shift = ((me * (length % LANES)) % LANES).astype(jnp.int32).reshape(1)
    own = shift_shard(shift, params, rows)
    if (outer, inner) == (4, 8):
        core = jnp.bitwise_and(jnp.right_shift(me, 3), 1)
        place = jnp.stack([me, core])
        got = {0: own}
        for node, kind in GATHER:
            got[node] = hop(got[node ^ HOPS[kind]], kind)
        pieces = [got[n] for n in GATHER_NODES]
        crossed = []
        for v in pieces:
            crossed.append(hop(v, "core"))
        cuts = [SCATTER_NODES[k : k + GROUP] for k in range(0, len(SCATTER_NODES), GROUP)]
        bo, lg, cg, blocks = run_step(
            devices, place, validity, latents, condition, cotangent, pieces + crossed,
            [[m] for m in near(GATHER_NODES) + far(GATHER_NODES)],
            [near(c) for c in cuts] + [far(c) for c in cuts],
        )
        sums = {}
        for j, cut in enumerate(cuts):
            theirs = hop(blocks[len(cuts) + j], "core")
            for k, node in enumerate(cut):
                sums[node] = (blocks[j][k].astype(F32) + theirs[k].astype(F32)).astype(BF)
        waiting = {n: [] for n in SCATTER_NODES}
        for node, kind in SCATTER:
            half = sums[node]
            if waiting[node]:
                half = half.astype(F32)
                for extra in waiting[node]:
                    half = half + extra.astype(F32)
                half = half.astype(BF)
            waiting[node ^ HOPS[kind]].append(hop(half, kind))
        parts = [sums[0]] + waiting[0]
    else:
        gathered = lax.all_gather(own, both, axis=0, tiled=False)
        every = [[(i, i) for i in range(devices)]]
        bo, lg, cg, (chunks,) = run_step(
            devices, jnp.zeros((2,), jnp.int32), validity, latents, condition, cotangent,
            [gathered], every, every,
        )
        parts = [lax.psum_scatter(chunks, both, scatter_dimension=0, tiled=False)]
    grad, squares = unshift(shift, parts, length)
    for axis, size in (("dp", outer), ("fsdp", inner)):
        d = 1
        while d < size:
            squares = squares + lax.ppermute(squares, axis, [(i, i ^ d) for i in range(size)])
            d *= 2
    clip_factor = jnp.minimum(1.0, MAX_NORM / (jnp.sqrt(squares[0, 0]) + NORM_EPS))
    grad_shard = grad.reshape(-1)[:length]
    clipped = grad_shard * clip_factor
    new_one = BETA_ONE * moment_one + (1.0 - BETA_ONE) * clipped
    new_two = BETA_TWO * moment_two + (1.0 - BETA_TWO) * clipped * clipped
    corrected_one = new_one / (1.0 - BETA_ONE**STEP)
    corrected_two = new_two / (1.0 - BETA_TWO**STEP)
    new_params = params - LEARN_RATE * (
        corrected_one / (jnp.sqrt(corrected_two) + ADAM_EPS) + WEIGHT_DECAY * params
    )
    return (
        bo.reshape(latents.shape), lg.reshape(latents.shape), cg,
        grad_shard, new_params, new_one, new_two,
    )


def solution(mesh):
    both = ("dp", "fsdp")
    in_specs = (
        P(both, None, None), P(both, None), P(both, None, None),
        P(both), P(both), P(both), P(both),
    )
    out_specs = (
        P(both, None, None), P(both, None, None), P(both, None),
        P(both), P(both), P(both), P(both),
    )
    return jax.shard_map(local, mesh=mesh, in_specs=in_specs, out_specs=out_specs, check_vma=False)
```

```python
import functools
import jax
import jax.numpy as jnp
from jax import lax
from jax.experimental import pallas as pl
from jax.experimental.pallas import tpu as pltpu
from jax.sharding import PartitionSpec as P


D = 384
FF = 1536
HEADS = 6
HEAD_DIM = 64
STEP = 3
LANES = 128

NORM_EPS = 1e-06
LEARN_RATE = 0.01
BETA_ONE = 0.9
BETA_TWO = 0.999
ADAM_EPS = 1e-08
WEIGHT_DECAY = 0.1
MAX_NORM = 1.0
GELU_COEF = 0.7978845608028654
CUBIC_COEF = 0.044715

VMEM_LIMIT = 48 * 1024 * 1024


BF = jnp.bfloat16
F32 = jnp.float32

ADA0 = 0
QKV0 = ADA0 + D * 6 * D // LANES
PROJ0 = QKV0 + D * 3 * D // LANES
FIRST0 = PROJ0 + D * D // LANES
SECOND0 = FIRST0 + D * FF // LANES
BIAS0 = SECOND0 + FF * D // LANES
BIAS_LEN = 6 * D + 3 * D + FF + D
TOTAL = BIAS0 * LANES + BIAS_LEN
B_ADA, B_QUERY, B_VALUE, B_PROJ, B_FIRST, B_SECOND = 0, 6 * D, 7 * D, 8 * D, 9 * D, 9 * D + FF

MATRICES = ((ADA0, D, 6 * D), (QKV0, D, 3 * D), (PROJ0, D, D), (FIRST0, D, FF), (SECOND0, FF, D))


def nn(a, b):
    return lax.dot_general(a, b, (((1,), (0,)), ((), ())), preferred_element_type=F32)


def nt(a, b):
    return lax.dot_general(a, b, (((1,), (1,)), ((), ())), preferred_element_type=F32)


def tn(a, b):
    return lax.dot_general(a, b, (((0,), (0,)), ((), ())), preferred_element_type=F32)


def silu(v):
    return v / (1.0 + jnp.exp(-v))


def mean_last(v):
    return jnp.sum(v, axis=-1, keepdims=True) * (1.0 / v.shape[-1])


def shard_geometry(devices):
    length = TOTAL // devices
    starts = [(length * i) // LANES for i in range(devices)]
    shifts = [(length * i) % LANES for i in range(devices)]
    counts = [-(-(shifts[i] + length) // LANES) for i in range(devices)]
    rows = -(-(max(counts) + 1) // 16) * 16
    return length, starts, shifts, counts, rows


def step_kernel(
    devices, seq, batch, slots_in, slots_out,
    me_ref, valid_ref, lat_hbm, cond_ref, cot_hbm, *rest,
):
    n_in = len(slots_in)
    pieces = rest[:n_in]
    bo_hbm, lg_hbm, cg_ref = rest[n_in : n_in + 3]
    n_out = len(slots_out)
    outs = rest[n_in + 3 : n_in + 3 + n_out]
    (
        stage, flat, w_ada, w_qkv, w_proj, w_first, w_second, bias,
        normed1, inv1, mixed1, qkv, probs, heads_f, heads_h, projected,
        middle, normed2, inv2, mixed2, slope, gelu_h, mlp_out,
        mod, gmod, gcol, gmlp_h, gpre_h, gmix, cond8, gmod_h,
        lat_ref, cot_ref, bo_ref, lg_ref, sem_lat, sem_cot, sem_bo, sem_lg,
    ) = rest[n_in + 3 + n_out :]
    gmid, gheads, gproj_h, gqkv_h = middle, mlp_out, gmlp_h, gpre_h
    _, starts, shifts, counts, rows = shard_geometry(devices)
    tokens = batch * seq
    scale = HEAD_DIM ** (-0.5)
    me = me_ref[0]
    core_one = me_ref[1] == 1

    def owner(masks):
        return jnp.bitwise_xor(me, jnp.where(core_one, masks[1], masks[0]))

    copy_lat = pltpu.make_async_copy(lat_hbm, lat_ref, sem_lat)
    copy_cot = pltpu.make_async_copy(cot_hbm, cot_ref, sem_cot)
    copy_bo = pltpu.make_async_copy(bo_ref, bo_hbm, sem_bo)
    copy_lg = pltpu.make_async_copy(lg_ref, lg_hbm, sem_lg)
    copy_lat.start()
    copy_cot.start()
    for ref, slots in zip(pieces, slots_in):
        for j, masks in enumerate(slots):
            stage[owner(masks)] = ref[...] if len(slots) == 1 else ref[j]

    chunk = 256

    def norm_one(i, carry):
        rs = pl.ds(pl.multiple_of(i * chunk, chunk), chunk)
        v = lat_ref[rs, :]
        cen = v - mean_last(v)
        inv = lax.rsqrt(mean_last(cen * cen) + NORM_EPS)
        normed1[rs, :] = cen * inv
        inv1[rs, :] = jnp.broadcast_to(inv, (chunk, LANES))
        return carry

    copy_lat.wait()
    lax.fori_loop(0, tokens // chunk, norm_one, 0)

    for i in range(devices):
        g = starts[i]
        n = counts[i]
        block = stage[i].astype(F32)
        if shifts[i] == 0:
            flat[g : g + n, :] = block[:n]
        else:
            flat[g : g + 1, :] = flat[g : g + 1, :] + block[:1]
            flat[g + 1 : g + n, :] = block[1:n]

    for w, (base, height, width) in zip((w_ada, w_qkv, w_proj, w_first, w_second), MATRICES):
        tiles = width // LANES
        for c in range(tiles):
            w[:, c * LANES : (c + 1) * LANES] = flat[pl.ds(base + c, height, stride=tiles), :].astype(BF)
    for r in range(BIAS_LEN // LANES):
        bias[:, r * LANES : (r + 1) * LANES] = flat[BIAS0 + r : BIAS0 + r + 1, :]

    cond8[...] = jnp.zeros_like(cond8)
    cond8[0:batch, :] = silu(cond_ref[...])
    ch = cond8[...].astype(BF)
    mod[...] = nn(ch, w_ada[...]) + bias[:, B_ADA : B_ADA + 6 * D]

    def part(ref, b, k):
        return ref[pl.ds(b, 1), k * D : (k + 1) * D]

    def mix_one(i, carry):
        b = i // (seq // chunk)
        rs = pl.ds(pl.multiple_of(i * chunk, chunk), chunk)
        mixed1[rs, :] = (normed1[rs, :] * (1.0 + part(mod, b, 1)) + part(mod, b, 0)).astype(BF)
        return carry

    lax.fori_loop(0, tokens // chunk, mix_one, 0)

    for j in range(3):
        cols = slice(j * D, (j + 1) * D)
        acc = nn(mixed1[...], w_qkv[:, cols])
        if j == 0:
            acc = acc + bias[:, B_QUERY : B_QUERY + D]
        if j == 2:
            acc = acc + bias[:, B_VALUE : B_VALUE + D]
        qkv[:, cols] = acc.astype(BF)

    lane = lax.broadcasted_iota(jnp.int32, (1, LANES), 1)
    low = lane < HEAD_DIM
    zero_bf = jnp.zeros((), BF)

    def keep(v, half):
        return jnp.where(low if half == 0 else jnp.logical_not(low), v, zero_bf)

    pairs = HEADS // 2

    def attn(b, carry):
        rs = pl.ds(pl.multiple_of(b * seq, seq), seq)
        for h in range(pairs):
            q = qkv[rs, h * LANES : (h + 1) * LANES]
            k = qkv[rs, D + h * LANES : D + (h + 1) * LANES]
            v = qkv[rs, 2 * D + h * LANES : 2 * D + (h + 1) * LANES]
            res = []
            for half in range(2):
                s = nt(keep(q, half), k) * scale
                e = jnp.exp(s - jnp.max(s, axis=-1, keepdims=True))
                p = e * (1.0 / jnp.sum(e, axis=-1, keepdims=True))
                probs[b * HEADS + 2 * h + half] = p
                res.append(nn(p.astype(BF), v))
            o = jnp.where(low, res[0], res[1])
            heads_f[rs, h * LANES : (h + 1) * LANES] = o
            heads_h[rs, h * LANES : (h + 1) * LANES] = o.astype(BF)
        return carry

    lax.fori_loop(0, batch, attn, 0)

    projected[...] = nn(heads_h[...], w_proj[...]) + bias[:, B_PROJ : B_PROJ + D]

    def mid(i, carry):
        b = i // (seq // chunk)
        rs = pl.ds(pl.multiple_of(i * chunk, chunk), chunk)
        m = lat_ref[rs, :] + part(mod, b, 2) * projected[rs, :]
        middle[rs, :] = m
        cen = m - mean_last(m)
        inv = lax.rsqrt(mean_last(cen * cen) + NORM_EPS)
        n2 = cen * inv
        normed2[rs, :] = n2
        inv2[rs, :] = jnp.broadcast_to(inv, (chunk, LANES))
        mixed2[rs, :] = (n2 * (1.0 + part(mod, b, 4)) + part(mod, b, 3)).astype(BF)
        return carry

    lax.fori_loop(0, tokens // chunk, mid, 0)

    fchunk = 256
    for j in range(FF // fchunk):
        cols = slice(j * fchunk, (j + 1) * fchunk)
        u = nn(mixed2[...], w_first[:, cols]) + bias[:, B_FIRST + j * fchunk : B_FIRST + (j + 1) * fchunk]
        uu = u * u
        t = jnp.tanh(GELU_COEF * (u + CUBIC_COEF * uu * u))
        half_u = 0.5 * u
        gelu_h[:, cols] = (half_u * (1.0 + t)).astype(BF)
        slope[:, cols] = 0.5 * (1.0 + t) + half_u * (1.0 - t * t) * GELU_COEF * (
            1.0 + 3.0 * CUBIC_COEF * uu
        )
    mlp_out[...] = nn(gelu_h[...], w_second[...]) + bias[:, B_SECOND : B_SECOND + D]

    gcol[...] = jnp.zeros_like(gcol)
    gmod[...] = jnp.zeros_like(gmod)

    def add_col(ref, b, k, v):
        ref[pl.ds(b, 1), k * D : (k + 1) * D] += jnp.sum(v, axis=0, keepdims=True)

    def out_step(i, carry):
        b = i // (seq // chunk)
        rs = pl.ds(pl.multiple_of(i * chunk, chunk), chunk)
        mo = mlp_out[rs, :]
        gate = part(mod, b, 5)
        bo_ref[rs, :] = middle[rs, :] + gate * mo
        up = cot_ref[rs, :] * valid_ref[b].astype(F32)
        add_col(gmod, b, 5, up * mo)
        gm = up * gate
        gcol[:, B_SECOND : B_SECOND + D] += jnp.sum(gm, axis=0, keepdims=True)
        gmlp_h[rs, :] = gm.astype(BF)
        return carry

    copy_cot.wait()
    lax.fori_loop(0, tokens // chunk, out_step, 0)
    copy_bo.start()

    def put(base, tiles, height, row0, c0, value):
        for c in range(value.shape[1] // LANES):
            flat[pl.ds(base + row0 * tiles + c0 + c, height, stride=tiles), :] = value[
                :, c * LANES : (c + 1) * LANES
            ]

    for j in range(FF // D):
        rr = slice(j * D, (j + 1) * D)
        put(SECOND0, D // LANES, D, j * D, 0, tn(gelu_h[:, rr], gmlp_h[...]))
    for j in range(FF // fchunk):
        cols = slice(j * fchunk, (j + 1) * fchunk)
        gp = nt(gmlp_h[...], w_second[cols, :]) * slope[:, cols]
        gcol[:, B_FIRST + j * fchunk : B_FIRST + (j + 1) * fchunk] = jnp.sum(gp, axis=0, keepdims=True)
        gpre_h[:, cols] = gp.astype(BF)
    for j in range(FF // D):
        cols = slice(j * D, (j + 1) * D)
        put(FIRST0, FF // LANES, D, 0, j * (D // LANES), tn(mixed2[...], gpre_h[:, cols]))
    gmix[...] = nt(gpre_h[...], w_first[...])

    def back_two(i, carry):
        b = i // (seq // chunk)
        rs = pl.ds(pl.multiple_of(i * chunk, chunk), chunk)
        g = gmix[rs, :]
        n2 = normed2[rs, :]
        add_col(gmod, b, 3, g)
        add_col(gmod, b, 4, g * n2)
        e = g * (1.0 + part(mod, b, 4))
        up = cot_ref[rs, :] * valid_ref[b].astype(F32)
        inv = inv2[rs, 0:1]
        gm = up + inv * (e - mean_last(e) - n2 * mean_last(e * n2))
        gmid[rs, :] = gm
        add_col(gmod, b, 2, gm * projected[rs, :])
        gp = gm * part(mod, b, 2)
        gcol[:, B_PROJ : B_PROJ + D] += jnp.sum(gp, axis=0, keepdims=True)
        gproj_h[rs, :] = gp.astype(BF)
        return carry

    lax.fori_loop(0, tokens // chunk, back_two, 0)

    put(PROJ0, D // LANES, D, 0, 0, tn(heads_h[...], gproj_h[...]))
    gheads[...] = nt(gproj_h[...], w_proj[...])

    def attn_back(b, carry):
        rs = pl.ds(pl.multiple_of(b * seq, seq), seq)
        for h in range(pairs):
            ls = slice(h * LANES, (h + 1) * LANES)
            q = qkv[rs, h * LANES : (h + 1) * LANES]
            k = qkv[rs, D + h * LANES : D + (h + 1) * LANES]
            v = qkv[rs, 2 * D + h * LANES : 2 * D + (h + 1) * LANES]
            gh = gheads[rs, ls]
            prod = gh * heads_f[rs, ls]
            ghh = gh.astype(BF)
            dq, dk, dv = [], [], []
            for half in range(2):
                delta = jnp.sum(
                    jnp.where(low if half == 0 else jnp.logical_not(low), prod, 0.0),
                    axis=-1, keepdims=True,
                )
                p = probs[b * HEADS + 2 * h + half]
                gp = nt(keep(ghh, half), v)
                gs = (p * (gp - delta)).astype(BF)
                dq.append(nn(gs, k))
                dk.append(tn(gs, q))
                dv.append(tn(p.astype(BF), ghh))
            gq = jnp.where(low, dq[0], dq[1]) * scale
            gk = jnp.where(low, dk[0], dk[1]) * scale
            gv = jnp.where(low, dv[0], dv[1])
            gcol[:, B_QUERY + h * LANES : B_QUERY + (h + 1) * LANES] += jnp.sum(gq, axis=0, keepdims=True)
            gcol[:, B_VALUE + h * LANES : B_VALUE + (h + 1) * LANES] += jnp.sum(gv, axis=0, keepdims=True)
            gqkv_h[rs, h * LANES : (h + 1) * LANES] = gq.astype(BF)
            gqkv_h[rs, D + h * LANES : D + (h + 1) * LANES] = gk.astype(BF)
            gqkv_h[rs, 2 * D + h * LANES : 2 * D + (h + 1) * LANES] = gv.astype(BF)
        return carry

    lax.fori_loop(0, batch, attn_back, 0)

    for j in range(3):
        cols = slice(j * D, (j + 1) * D)
        put(QKV0, 3 * D // LANES, D, 0, j * (D // LANES), tn(mixed1[...], gqkv_h[:, cols]))
    gmix[...] = nt(gqkv_h[:, : 3 * D], w_qkv[...])

    def back_one(i, carry):
        b = i // (seq // chunk)
        rs = pl.ds(pl.multiple_of(i * chunk, chunk), chunk)
        g = gmix[rs, :]
        n1 = normed1[rs, :]
        add_col(gmod, b, 0, g)
        add_col(gmod, b, 1, g * n1)
        e = g * (1.0 + part(mod, b, 1))
        inv = inv1[rs, 0:1]
        lg_ref[rs, :] = gmid[rs, :] + inv * (e - mean_last(e) - n1 * mean_last(e * n1))
        return carry

    lax.fori_loop(0, tokens // chunk, back_one, 0)
    copy_lg.start()

    gmod_h[...] = gmod[...].astype(BF)
    for j in range(6):
        cols = slice(j * D, (j + 1) * D)
        put(ADA0, 6 * D // LANES, D, 0, j * (D // LANES), tn(ch, gmod_h[:, cols]))
    gcol[:, B_ADA : B_ADA + 6 * D] = jnp.sum(gmod[...], axis=0, keepdims=True)
    cg = nt(gmod_h[...], w_ada[...])[0:batch]
    cv = cond_ref[...]
    sig = 1.0 / (1.0 + jnp.exp(-cv))
    cg_ref[...] = cg * (sig * (1.0 + cv * (1.0 - sig)))

    for r in range(BIAS_LEN // LANES):
        flat[BIAS0 + r : BIAS0 + r + 1, :] = gcol[:, r * LANES : (r + 1) * LANES]

    for i in range(devices):
        g = starts[i]
        stage[i] = flat[g : g + rows, :].astype(BF)
    for ref, slots in zip(outs, slots_out):
        for j, masks in enumerate(slots):
            ref[j] = stage[owner(masks)]
    copy_bo.wait()
    copy_lg.wait()


def run_step(
    devices, place, validity, latents, condition, cotangent, pieces, slots_in, slots_out
):
    batch, seq, _ = latents.shape
    tokens = batch * seq
    _, starts, _, _, rows = shard_geometry(devices)
    flat_rows = -(-(starts[-1] + rows) // 16) * 16
    vm = pl.BlockSpec(memory_space=pltpu.VMEM)
    hb = pl.BlockSpec(memory_space=pl.ANY)
    sm = pl.BlockSpec(memory_space=pltpu.SMEM)
    out_shape = [
        jax.ShapeDtypeStruct((tokens, D), F32),
        jax.ShapeDtypeStruct((tokens, D), F32),
        jax.ShapeDtypeStruct((batch, D), F32),
    ] + [
        pltpu.VMEM((len(slots), rows, LANES), BF) for slots in slots_out
    ]
    V = pltpu.VMEM
    scratch = [
        V((devices, rows, LANES), BF),
        V((flat_rows, LANES), F32),
        V((D, 6 * D), BF), V((D, 3 * D), BF), V((D, D), BF), V((D, FF), BF), V((FF, D), BF),
        V((1, BIAS_LEN), F32),
        V((tokens, D), F32), V((tokens, LANES), F32), V((tokens, D), BF), V((tokens, 3 * D), BF),
        V((batch * HEADS, seq, seq), F32), V((tokens, D), F32), V((tokens, D), BF), V((tokens, D), F32),
        V((tokens, D), F32), V((tokens, D), F32), V((tokens, LANES), F32), V((tokens, D), BF),
        V((tokens, FF), F32), V((tokens, FF), BF), V((tokens, D), F32),
        V((8, 6 * D), F32), V((8, 6 * D), F32), V((1, BIAS_LEN), F32),
        V((tokens, D), BF), V((tokens, FF), BF), V((tokens, D), F32), V((8, D), F32), V((8, 6 * D), BF),
        V((tokens, D), F32), V((tokens, D), F32), V((tokens, D), F32), V((tokens, D), F32),
        pltpu.SemaphoreType.DMA, pltpu.SemaphoreType.DMA, pltpu.SemaphoreType.DMA, pltpu.SemaphoreType.DMA,
    ]
    body = functools.partial(step_kernel, devices, seq, batch, slots_in, slots_out)
    res = pl.pallas_call(
        body,
        out_shape=out_shape,
        in_specs=[sm, sm, hb, vm, hb] + [vm] * len(pieces),
        out_specs=[hb, hb, vm] + [vm] * len(slots_out),
        scratch_shapes=scratch,
        compiler_params=pltpu.CompilerParams(vmem_limit_bytes=VMEM_LIMIT),
        name="step",
    )(
        place, validity, latents.reshape(tokens, D), condition, cotangent.reshape(tokens, D),
        *[pltpu.with_memory_space_constraint(p, pltpu.VMEM) for p in pieces],
    )
    return res[0], res[1], res[2], res[3:]


def shift_kernel(s_ref, x_ref, o_ref):
    s = s_ref[0]
    rolled = pltpu.roll(x_ref[...], s, 1)
    above = pltpu.roll(rolled, 1, 0)
    lane = lax.broadcasted_iota(jnp.int32, rolled.shape, 1)
    o_ref[...] = jnp.where(lane < s, above, rolled).astype(BF)


def shift_shard(shift, params, rows):
    padded = jnp.pad(params, (0, rows * LANES - params.shape[0])).reshape(rows, LANES)
    return pl.pallas_call(
        shift_kernel,
        out_shape=jax.ShapeDtypeStruct((rows, LANES), BF),
        in_specs=[pl.BlockSpec(memory_space=pltpu.SMEM), pl.BlockSpec(memory_space=pltpu.VMEM)],
        out_specs=pl.BlockSpec(memory_space=pltpu.VMEM),
        name="shift",
    )(shift, padded)


def unshift_kernel(length, n, s_ref, *refs):
    s = s_ref[0]
    total = refs[0][...].astype(F32)
    for r in refs[1:n]:
        total = total + r[...].astype(F32)
    g_ref, sq_ref = refs[n:]
    rows = total.shape[0]
    back = jnp.where(s == 0, 0, LANES - s)
    rolled = pltpu.roll(total, back, 1)
    below = pltpu.roll(rolled, rows - 1, 0)
    lane = lax.broadcasted_iota(jnp.int32, rolled.shape, 1)
    row = lax.broadcasted_iota(jnp.int32, rolled.shape, 0)
    out = jnp.where(lane < LANES - s, rolled, below)
    out = jnp.where(row * LANES + lane < length, out, 0.0)
    g_ref[...] = out
    sq_ref[...] = jnp.full(sq_ref.shape, jnp.sum(out * out), F32)


def unshift(shift, parts, length):
    rows = parts[0].shape[0]
    return pl.pallas_call(
        functools.partial(unshift_kernel, length, len(parts)),
        out_shape=[jax.ShapeDtypeStruct((rows, LANES), F32), jax.ShapeDtypeStruct((8, LANES), F32)],
        in_specs=[pl.BlockSpec(memory_space=pltpu.SMEM)]
        + [pl.BlockSpec(memory_space=pltpu.VMEM)] * len(parts),
        out_specs=[pl.BlockSpec(memory_space=pltpu.VMEM)] * 2,
        name="unshift",
    )(shift, *parts)


HOPS = {"a": 16, "b": 1, "z1": 2, "z2": 4, "z3": 6}
GATHER = (
    (16, "a"), (4, "z2"), (1, "b"), (2, "z1"), (18, "z1"), (22, "z3"), (17, "a"), (7, "z3"),
    (5, "b"), (20, "a"), (19, "z1"), (3, "b"), (21, "a"), (6, "z1"), (23, "b"),
)
SCATTER = (
    (23, "z3"), (20, "a"), (7, "z1"), (21, "a"), (3, "b"), (19, "z1"), (6, "z1"), (22, "z3"),
    (5, "b"), (18, "a"), (17, "b"), (4, "z2"), (2, "z1"), (1, "b"), (16, "a"),
)
GATHER_NODES = (0,) + tuple(n for n, _ in GATHER)
SCATTER_NODES = tuple(n for n, _ in SCATTER) + (0,)
GROUP = 4


def swap(node):
    return (node & 6) | (16 if node & 1 else 0) | (1 if node & 16 else 0)


def hop(v, kind):
    pairs = []
    for i in range(32):
        m = 8 if kind == "core" else HOPS[kind]
        pairs.append((i, i ^ (swap(m) if i & 8 and kind != "core" else m)))
    return lax.ppermute(v, ("dp", "fsdp"), pairs)


def near(nodes):
    return [(n, swap(n)) for n in nodes]


def far(nodes):
    return [(8 ^ swap(n), 8 ^ n) for n in nodes]


def local(latents, condition, cotangent, validity, params, moment_one, moment_two):
    outer = lax.axis_size("dp")
    inner = lax.axis_size("fsdp")
    devices = outer * inner
    both = ("dp", "fsdp")
    me = (lax.axis_index("dp") * inner + lax.axis_index("fsdp")).astype(jnp.int32)
    length, _, _, _, rows = shard_geometry(devices)
    shift = ((me * (length % LANES)) % LANES).astype(jnp.int32).reshape(1)
    own = shift_shard(shift, params, rows)
    if (outer, inner) == (4, 8):
        core = jnp.bitwise_and(jnp.right_shift(me, 3), 1)
        place = jnp.stack([me, core])
        got = {0: own}
        for node, kind in GATHER:
            got[node] = hop(got[node ^ HOPS[kind]], kind)
        pieces = [got[n] for n in GATHER_NODES]
        crossed = []
        for v in pieces:
            crossed.append(hop(v, "core"))
        cuts = [SCATTER_NODES[k : k + GROUP] for k in range(0, len(SCATTER_NODES), GROUP)]
        bo, lg, cg, blocks = run_step(
            devices, place, validity, latents, condition, cotangent, pieces + crossed,
            [[m] for m in near(GATHER_NODES) + far(GATHER_NODES)],
            [near(c) for c in cuts] + [far(c) for c in cuts],
        )
        sums = {}
        for j, cut in enumerate(cuts):
            theirs = hop(blocks[len(cuts) + j], "core")
            for k, node in enumerate(cut):
                sums[node] = (blocks[j][k].astype(F32) + theirs[k].astype(F32)).astype(BF)
        waiting = {n: [] for n in SCATTER_NODES}
        for node, kind in SCATTER:
            half = sums[node]
            if waiting[node]:
                half = half.astype(F32)
                for extra in waiting[node]:
                    half = half + extra.astype(F32)
                half = half.astype(BF)
            waiting[node ^ HOPS[kind]].append(hop(half, kind))
        parts = [sums[0]] + waiting[0]
    else:
        gathered = lax.all_gather(own, both, axis=0, tiled=False)
        every = [[(i, i) for i in range(devices)]]
        bo, lg, cg, (chunks,) = run_step(
            devices, jnp.zeros((2,), jnp.int32), validity, latents, condition, cotangent,
            [gathered], every, every,
        )
        parts = [lax.psum_scatter(chunks, both, scatter_dimension=0, tiled=False)]
    grad, squares = unshift(shift, parts, length)
    if (outer, inner) == (4, 8):
        rounds = ((8,), (16, 1, 17), (2, 4, 6))
    else:
        rounds = tuple((1 << k,) for k in range((devices - 1).bit_length()))
    for masks in rounds:
        came = [lax.ppermute(squares, both, [(i, i ^ m) for i in range(devices)]) for m in masks]
        for v in came:
            squares = squares + v
    clip_factor = jnp.minimum(1.0, MAX_NORM / (jnp.sqrt(squares[0, 0]) + NORM_EPS))
    grad_shard = grad.reshape(-1)[:length]
    clipped = grad_shard * clip_factor
    new_one = BETA_ONE * moment_one + (1.0 - BETA_ONE) * clipped
    new_two = BETA_TWO * moment_two + (1.0 - BETA_TWO) * clipped * clipped
    corrected_one = new_one / (1.0 - BETA_ONE**STEP)
    corrected_two = new_two / (1.0 - BETA_TWO**STEP)
    new_params = params - LEARN_RATE * (
        corrected_one / (jnp.sqrt(corrected_two) + ADAM_EPS) + WEIGHT_DECAY * params
    )
    return (
        bo.reshape(latents.shape), lg.reshape(latents.shape), cg,
        grad_shard, new_params, new_one, new_two,
    )


def solution(mesh):
    both = ("dp", "fsdp")
    in_specs = (
        P(both, None, None), P(both, None), P(both, None, None),
        P(both), P(both), P(both), P(both),
    )
    out_specs = (
        P(both, None, None), P(both, None, None), P(both, None),
        P(both), P(both), P(both), P(both),
    )
    return jax.shard_map(local, mesh=mesh, in_specs=in_specs, out_specs=out_specs, check_vma=False)
```

```python
import functools
import jax
import jax.numpy as jnp
from jax import lax
from jax.experimental import pallas as pl
from jax.experimental.pallas import tpu as pltpu
from jax.sharding import PartitionSpec as P


D = 384
FF = 1536
HEADS = 6
HEAD_DIM = 64
STEP = 3
LANES = 128

NORM_EPS = 1e-06
LEARN_RATE = 0.01
BETA_ONE = 0.9
BETA_TWO = 0.999
ADAM_EPS = 1e-08
WEIGHT_DECAY = 0.1
MAX_NORM = 1.0
GELU_COEF = 0.7978845608028654
CUBIC_COEF = 0.044715

VMEM_LIMIT = 48 * 1024 * 1024


BF = jnp.bfloat16
F32 = jnp.float32

ADA0 = 0
QKV0 = ADA0 + D * 6 * D // LANES
PROJ0 = QKV0 + D * 3 * D // LANES
FIRST0 = PROJ0 + D * D // LANES
SECOND0 = FIRST0 + D * FF // LANES
BIAS0 = SECOND0 + FF * D // LANES
BIAS_LEN = 6 * D + 3 * D + FF + D
TOTAL = BIAS0 * LANES + BIAS_LEN
B_ADA, B_QUERY, B_VALUE, B_PROJ, B_FIRST, B_SECOND = 0, 6 * D, 7 * D, 8 * D, 9 * D, 9 * D + FF

MATRICES = ((ADA0, D, 6 * D), (QKV0, D, 3 * D), (PROJ0, D, D), (FIRST0, D, FF), (SECOND0, FF, D))


def nn(a, b):
    return lax.dot_general(a, b, (((1,), (0,)), ((), ())), preferred_element_type=F32)


def nt(a, b):
    return lax.dot_general(a, b, (((1,), (1,)), ((), ())), preferred_element_type=F32)


def tn(a, b):
    return lax.dot_general(a, b, (((0,), (0,)), ((), ())), preferred_element_type=F32)


def silu(v):
    return v / (1.0 + jnp.exp(-v))


def mean_last(v):
    return jnp.sum(v, axis=-1, keepdims=True) * (1.0 / v.shape[-1])


def shard_geometry(devices):
    length = TOTAL // devices
    starts = [(length * i) // LANES for i in range(devices)]
    shifts = [(length * i) % LANES for i in range(devices)]
    counts = [-(-(shifts[i] + length) // LANES) for i in range(devices)]
    rows = -(-(max(counts) + 1) // 16) * 16
    return length, starts, shifts, counts, rows


def step_kernel(
    devices, seq, batch, slots_in, slots_out,
    me_ref, valid_ref, lat_hbm, cond_ref, cot_hbm, *rest,
):
    n_in = len(slots_in)
    pieces = rest[:n_in]
    bo_hbm, lg_hbm, cg_ref = rest[n_in : n_in + 3]
    n_out = len(slots_out)
    outs = rest[n_in + 3 : n_in + 3 + n_out]
    (
        stage, flat, w_ada, w_qkv, w_proj, w_first, w_second, bias,
        normed1, inv1, mixed1, qkv, probs, heads_f, heads_h, projected,
        middle, normed2, inv2, mixed2, slope, gelu_h, mlp_out,
        mod, gmod, gcol, gmlp_h, gpre_h, gmix, cond8, gmod_h,
        lat_ref, cot_ref, bo_ref, lg_ref, sem_lat, sem_cot, sem_bo, sem_lg,
    ) = rest[n_in + 3 + n_out :]
    gmid, gheads, gproj_h, gqkv_h = middle, mlp_out, gmlp_h, gpre_h
    _, starts, shifts, counts, rows = shard_geometry(devices)
    tokens = batch * seq
    scale = HEAD_DIM ** (-0.5)
    me = me_ref[0]
    core_one = me_ref[1] == 1

    def owner(masks):
        return jnp.bitwise_xor(me, jnp.where(core_one, masks[1], masks[0]))

    copy_lat = pltpu.make_async_copy(lat_hbm, lat_ref, sem_lat)
    copy_cot = pltpu.make_async_copy(cot_hbm, cot_ref, sem_cot)
    copy_bo = pltpu.make_async_copy(bo_ref, bo_hbm, sem_bo)
    copy_lg = pltpu.make_async_copy(lg_ref, lg_hbm, sem_lg)
    copy_lat.start()
    copy_cot.start()
    for ref, slots in zip(pieces, slots_in):
        for j, masks in enumerate(slots):
            stage[owner(masks)] = ref[...] if len(slots) == 1 else ref[j]

    chunk = 256

    def norm_one(i, carry):
        rs = pl.ds(pl.multiple_of(i * chunk, chunk), chunk)
        v = lat_ref[rs, :]
        cen = v - mean_last(v)
        inv = lax.rsqrt(mean_last(cen * cen) + NORM_EPS)
        normed1[rs, :] = cen * inv
        inv1[rs, :] = jnp.broadcast_to(inv, (chunk, LANES))
        return carry

    copy_lat.wait()
    lax.fori_loop(0, tokens // chunk, norm_one, 0)

    for i in range(devices):
        g = starts[i]
        n = counts[i]
        block = stage[i].astype(F32)
        if shifts[i] == 0:
            flat[g : g + n, :] = block[:n]
        else:
            flat[g : g + 1, :] = flat[g : g + 1, :] + block[:1]
            flat[g + 1 : g + n, :] = block[1:n]

    for w, (base, height, width) in zip((w_ada, w_qkv, w_proj, w_first, w_second), MATRICES):
        tiles = width // LANES
        for c in range(tiles):
            w[:, c * LANES : (c + 1) * LANES] = flat[pl.ds(base + c, height, stride=tiles), :].astype(BF)
    for r in range(BIAS_LEN // LANES):
        bias[:, r * LANES : (r + 1) * LANES] = flat[BIAS0 + r : BIAS0 + r + 1, :]

    cond8[...] = jnp.zeros_like(cond8)
    cond8[0:batch, :] = silu(cond_ref[...])
    ch = cond8[...].astype(BF)
    mod[...] = nn(ch, w_ada[...]) + bias[:, B_ADA : B_ADA + 6 * D]

    def part(ref, b, k):
        return ref[pl.ds(b, 1), k * D : (k + 1) * D]

    def mix_one(i, carry):
        b = i // (seq // chunk)
        rs = pl.ds(pl.multiple_of(i * chunk, chunk), chunk)
        mixed1[rs, :] = (normed1[rs, :] * (1.0 + part(mod, b, 1)) + part(mod, b, 0)).astype(BF)
        return carry

    lax.fori_loop(0, tokens // chunk, mix_one, 0)

    for j in range(3):
        cols = slice(j * D, (j + 1) * D)
        acc = nn(mixed1[...], w_qkv[:, cols])
        if j == 0:
            acc = acc + bias[:, B_QUERY : B_QUERY + D]
        if j == 2:
            acc = acc + bias[:, B_VALUE : B_VALUE + D]
        qkv[:, cols] = acc.astype(BF)

    lane = lax.broadcasted_iota(jnp.int32, (1, LANES), 1)
    low = lane < HEAD_DIM
    zero_bf = jnp.zeros((), BF)

    def keep(v, half):
        return jnp.where(low if half == 0 else jnp.logical_not(low), v, zero_bf)

    pairs = HEADS // 2

    def attn(b, carry):
        rs = pl.ds(pl.multiple_of(b * seq, seq), seq)
        for h in range(pairs):
            q = qkv[rs, h * LANES : (h + 1) * LANES]
            k = qkv[rs, D + h * LANES : D + (h + 1) * LANES]
            v = qkv[rs, 2 * D + h * LANES : 2 * D + (h + 1) * LANES]
            res = []
            for half in range(2):
                s = nt(keep(q, half), k) * scale
                e = jnp.exp(s - jnp.max(s, axis=-1, keepdims=True))
                p = e * (1.0 / jnp.sum(e, axis=-1, keepdims=True))
                probs[b * HEADS + 2 * h + half] = p
                res.append(nn(p.astype(BF), v))
            o = jnp.where(low, res[0], res[1])
            heads_f[rs, h * LANES : (h + 1) * LANES] = o
            heads_h[rs, h * LANES : (h + 1) * LANES] = o.astype(BF)
        return carry

    lax.fori_loop(0, batch, attn, 0)

    projected[...] = nn(heads_h[...], w_proj[...]) + bias[:, B_PROJ : B_PROJ + D]

    def mid(i, carry):
        b = i // (seq // chunk)
        rs = pl.ds(pl.multiple_of(i * chunk, chunk), chunk)
        m = lat_ref[rs, :] + part(mod, b, 2) * projected[rs, :]
        middle[rs, :] = m
        cen = m - mean_last(m)
        inv = lax.rsqrt(mean_last(cen * cen) + NORM_EPS)
        n2 = cen * inv
        normed2[rs, :] = n2
        inv2[rs, :] = jnp.broadcast_to(inv, (chunk, LANES))
        mixed2[rs, :] = (n2 * (1.0 + part(mod, b, 4)) + part(mod, b, 3)).astype(BF)
        return carry

    lax.fori_loop(0, tokens // chunk, mid, 0)

    fchunk = 256
    for j in range(FF // fchunk):
        cols = slice(j * fchunk, (j + 1) * fchunk)
        u = nn(mixed2[...], w_first[:, cols]) + bias[:, B_FIRST + j * fchunk : B_FIRST + (j + 1) * fchunk]
        uu = u * u
        t = jnp.tanh(GELU_COEF * (u + CUBIC_COEF * uu * u))
        half_u = 0.5 * u
        gelu_h[:, cols] = (half_u * (1.0 + t)).astype(BF)
        slope[:, cols] = 0.5 * (1.0 + t) + half_u * (1.0 - t * t) * GELU_COEF * (
            1.0 + 3.0 * CUBIC_COEF * uu
        )
    mlp_out[...] = nn(gelu_h[...], w_second[...]) + bias[:, B_SECOND : B_SECOND + D]

    gcol[...] = jnp.zeros_like(gcol)
    gmod[...] = jnp.zeros_like(gmod)

    def add_col(ref, b, k, v):
        ref[pl.ds(b, 1), k * D : (k + 1) * D] += jnp.sum(v, axis=0, keepdims=True)

    def out_step(i, carry):
        b = i // (seq // chunk)
        rs = pl.ds(pl.multiple_of(i * chunk, chunk), chunk)
        mo = mlp_out[rs, :]
        gate = part(mod, b, 5)
        bo_ref[rs, :] = middle[rs, :] + gate * mo
        up = cot_ref[rs, :] * valid_ref[b].astype(F32)
        add_col(gmod, b, 5, up * mo)
        gm = up * gate
        gcol[:, B_SECOND : B_SECOND + D] += jnp.sum(gm, axis=0, keepdims=True)
        gmlp_h[rs, :] = gm.astype(BF)
        return carry

    copy_cot.wait()
    lax.fori_loop(0, tokens // chunk, out_step, 0)
    copy_bo.start()

    def put(base, tiles, height, row0, c0, value):
        for c in range(value.shape[1] // LANES):
            flat[pl.ds(base + row0 * tiles + c0 + c, height, stride=tiles), :] = value[
                :, c * LANES : (c + 1) * LANES
            ]

    for j in range(FF // D):
        rr = slice(j * D, (j + 1) * D)
        put(SECOND0, D // LANES, D, j * D, 0, tn(gelu_h[:, rr], gmlp_h[...]))
    for j in range(FF // fchunk):
        cols = slice(j * fchunk, (j + 1) * fchunk)
        gp = nt(gmlp_h[...], w_second[cols, :]) * slope[:, cols]
        gcol[:, B_FIRST + j * fchunk : B_FIRST + (j + 1) * fchunk] = jnp.sum(gp, axis=0, keepdims=True)
        gpre_h[:, cols] = gp.astype(BF)
    for j in range(FF // D):
        cols = slice(j * D, (j + 1) * D)
        put(FIRST0, FF // LANES, D, 0, j * (D // LANES), tn(mixed2[...], gpre_h[:, cols]))
    gmix[...] = nt(gpre_h[...], w_first[...])

    def back_two(i, carry):
        b = i // (seq // chunk)
        rs = pl.ds(pl.multiple_of(i * chunk, chunk), chunk)
        g = gmix[rs, :]
        n2 = normed2[rs, :]
        add_col(gmod, b, 3, g)
        add_col(gmod, b, 4, g * n2)
        e = g * (1.0 + part(mod, b, 4))
        up = cot_ref[rs, :] * valid_ref[b].astype(F32)
        inv = inv2[rs, 0:1]
        gm = up + inv * (e - mean_last(e) - n2 * mean_last(e * n2))
        gmid[rs, :] = gm
        add_col(gmod, b, 2, gm * projected[rs, :])
        gp = gm * part(mod, b, 2)
        gcol[:, B_PROJ : B_PROJ + D] += jnp.sum(gp, axis=0, keepdims=True)
        gproj_h[rs, :] = gp.astype(BF)
        return carry

    lax.fori_loop(0, tokens // chunk, back_two, 0)

    put(PROJ0, D // LANES, D, 0, 0, tn(heads_h[...], gproj_h[...]))
    gheads[...] = nt(gproj_h[...], w_proj[...])

    def attn_back(b, carry):
        rs = pl.ds(pl.multiple_of(b * seq, seq), seq)
        for h in range(pairs):
            ls = slice(h * LANES, (h + 1) * LANES)
            q = qkv[rs, h * LANES : (h + 1) * LANES]
            k = qkv[rs, D + h * LANES : D + (h + 1) * LANES]
            v = qkv[rs, 2 * D + h * LANES : 2 * D + (h + 1) * LANES]
            gh = gheads[rs, ls]
            prod = gh * heads_f[rs, ls]
            ghh = gh.astype(BF)
            dq, dk, dv = [], [], []
            for half in range(2):
                delta = jnp.sum(
                    jnp.where(low if half == 0 else jnp.logical_not(low), prod, 0.0),
                    axis=-1, keepdims=True,
                )
                p = probs[b * HEADS + 2 * h + half]
                gp = nt(keep(ghh, half), v)
                gs = (p * (gp - delta)).astype(BF)
                dq.append(nn(gs, k))
                dk.append(tn(gs, q))
                dv.append(tn(p.astype(BF), ghh))
            gq = jnp.where(low, dq[0], dq[1]) * scale
            gk = jnp.where(low, dk[0], dk[1]) * scale
            gv = jnp.where(low, dv[0], dv[1])
            gcol[:, B_QUERY + h * LANES : B_QUERY + (h + 1) * LANES] += jnp.sum(gq, axis=0, keepdims=True)
            gcol[:, B_VALUE + h * LANES : B_VALUE + (h + 1) * LANES] += jnp.sum(gv, axis=0, keepdims=True)
            gqkv_h[rs, h * LANES : (h + 1) * LANES] = gq.astype(BF)
            gqkv_h[rs, D + h * LANES : D + (h + 1) * LANES] = gk.astype(BF)
            gqkv_h[rs, 2 * D + h * LANES : 2 * D + (h + 1) * LANES] = gv.astype(BF)
        return carry

    lax.fori_loop(0, batch, attn_back, 0)

    for j in range(3):
        cols = slice(j * D, (j + 1) * D)
        put(QKV0, 3 * D // LANES, D, 0, j * (D // LANES), tn(mixed1[...], gqkv_h[:, cols]))
    gmix[...] = nt(gqkv_h[:, : 3 * D], w_qkv[...])

    def back_one(i, carry):
        b = i // (seq // chunk)
        rs = pl.ds(pl.multiple_of(i * chunk, chunk), chunk)
        g = gmix[rs, :]
        n1 = normed1[rs, :]
        add_col(gmod, b, 0, g)
        add_col(gmod, b, 1, g * n1)
        e = g * (1.0 + part(mod, b, 1))
        inv = inv1[rs, 0:1]
        lg_ref[rs, :] = gmid[rs, :] + inv * (e - mean_last(e) - n1 * mean_last(e * n1))
        return carry

    lax.fori_loop(0, tokens // chunk, back_one, 0)
    copy_lg.start()

    gmod_h[...] = gmod[...].astype(BF)
    for j in range(6):
        cols = slice(j * D, (j + 1) * D)
        put(ADA0, 6 * D // LANES, D, 0, j * (D // LANES), tn(ch, gmod_h[:, cols]))
    gcol[:, B_ADA : B_ADA + 6 * D] = jnp.sum(gmod[...], axis=0, keepdims=True)
    cg = nt(gmod_h[...], w_ada[...])[0:batch]
    cv = cond_ref[...]
    sig = 1.0 / (1.0 + jnp.exp(-cv))
    cg_ref[...] = cg * (sig * (1.0 + cv * (1.0 - sig)))

    for r in range(BIAS_LEN // LANES):
        flat[BIAS0 + r : BIAS0 + r + 1, :] = gcol[:, r * LANES : (r + 1) * LANES]

    for i in range(devices):
        g = starts[i]
        stage[i] = flat[g : g + rows, :].astype(BF)
    for ref, slots in zip(outs, slots_out):
        for j, masks in enumerate(slots):
            ref[j] = stage[owner(masks)]
    copy_bo.wait()
    copy_lg.wait()


def run_step(
    devices, place, validity, latents, condition, cotangent, pieces, slots_in, slots_out
):
    batch, seq, _ = latents.shape
    tokens = batch * seq
    _, starts, _, _, rows = shard_geometry(devices)
    flat_rows = -(-(starts[-1] + rows) // 16) * 16
    vm = pl.BlockSpec(memory_space=pltpu.VMEM)
    hb = pl.BlockSpec(memory_space=pl.ANY)
    sm = pl.BlockSpec(memory_space=pltpu.SMEM)
    out_shape = [
        jax.ShapeDtypeStruct((tokens, D), F32),
        jax.ShapeDtypeStruct((tokens, D), F32),
        jax.ShapeDtypeStruct((batch, D), F32),
    ] + [
        pltpu.VMEM((len(slots), rows, LANES), BF) for slots in slots_out
    ]
    V = pltpu.VMEM
    scratch = [
        V((devices, rows, LANES), BF),
        V((flat_rows, LANES), F32),
        V((D, 6 * D), BF), V((D, 3 * D), BF), V((D, D), BF), V((D, FF), BF), V((FF, D), BF),
        V((1, BIAS_LEN), F32),
        V((tokens, D), F32), V((tokens, LANES), F32), V((tokens, D), BF), V((tokens, 3 * D), BF),
        V((batch * HEADS, seq, seq), F32), V((tokens, D), F32), V((tokens, D), BF), V((tokens, D), F32),
        V((tokens, D), F32), V((tokens, D), F32), V((tokens, LANES), F32), V((tokens, D), BF),
        V((tokens, FF), F32), V((tokens, FF), BF), V((tokens, D), F32),
        V((8, 6 * D), F32), V((8, 6 * D), F32), V((1, BIAS_LEN), F32),
        V((tokens, D), BF), V((tokens, FF), BF), V((tokens, D), F32), V((8, D), F32), V((8, 6 * D), BF),
        V((tokens, D), F32), V((tokens, D), F32), V((tokens, D), F32), V((tokens, D), F32),
        pltpu.SemaphoreType.DMA, pltpu.SemaphoreType.DMA, pltpu.SemaphoreType.DMA, pltpu.SemaphoreType.DMA,
    ]
    body = functools.partial(step_kernel, devices, seq, batch, slots_in, slots_out)
    res = pl.pallas_call(
        body,
        out_shape=out_shape,
        in_specs=[sm, sm, hb, vm, hb] + [vm] * len(pieces),
        out_specs=[hb, hb, vm] + [vm] * len(slots_out),
        scratch_shapes=scratch,
        compiler_params=pltpu.CompilerParams(vmem_limit_bytes=VMEM_LIMIT),
        name="step",
    )(
        place, validity, latents.reshape(tokens, D), condition, cotangent.reshape(tokens, D),
        *[pltpu.with_memory_space_constraint(p, pltpu.VMEM) for p in pieces],
    )
    return res[0], res[1], res[2], res[3:]


def shift_kernel(s_ref, x_ref, o_ref):
    s = s_ref[0]
    rolled = pltpu.roll(x_ref[...], s, 1)
    above = pltpu.roll(rolled, 1, 0)
    lane = lax.broadcasted_iota(jnp.int32, rolled.shape, 1)
    o_ref[...] = jnp.where(lane < s, above, rolled).astype(BF)


def shift_shard(shift, params, rows):
    padded = jnp.pad(params, (0, rows * LANES - params.shape[0])).reshape(rows, LANES)
    return pl.pallas_call(
        shift_kernel,
        out_shape=pltpu.VMEM((rows, LANES), BF),
        in_specs=[pl.BlockSpec(memory_space=pltpu.SMEM), pl.BlockSpec(memory_space=pltpu.VMEM)],
        out_specs=pl.BlockSpec(memory_space=pltpu.VMEM),
        name="shift",
    )(shift, pltpu.with_memory_space_constraint(padded, pltpu.VMEM))


def unshift_kernel(length, n, s_ref, *refs):
    s = s_ref[0]
    total = refs[0][...].astype(F32)
    for r in refs[1:n]:
        total = total + r[...].astype(F32)
    g_ref, sq_ref = refs[n:]
    rows = total.shape[0]
    back = jnp.where(s == 0, 0, LANES - s)
    rolled = pltpu.roll(total, back, 1)
    below = pltpu.roll(rolled, rows - 1, 0)
    lane = lax.broadcasted_iota(jnp.int32, rolled.shape, 1)
    row = lax.broadcasted_iota(jnp.int32, rolled.shape, 0)
    out = jnp.where(lane < LANES - s, rolled, below)
    out = jnp.where(row * LANES + lane < length, out, 0.0)
    g_ref[...] = out
    sq_ref[...] = jnp.full(sq_ref.shape, jnp.sum(out * out), F32)


def unshift(shift, parts, length):
    rows = parts[0].shape[0]
    return pl.pallas_call(
        functools.partial(unshift_kernel, length, len(parts)),
        out_shape=[pltpu.VMEM((rows, LANES), F32), pltpu.VMEM((8, LANES), F32)],
        in_specs=[pl.BlockSpec(memory_space=pltpu.SMEM)]
        + [pl.BlockSpec(memory_space=pltpu.VMEM)] * len(parts),
        out_specs=[pl.BlockSpec(memory_space=pltpu.VMEM)] * 2,
        name="unshift",
    )(shift, *[pltpu.with_memory_space_constraint(p, pltpu.VMEM) for p in parts])


HOPS = {"a": 16, "b": 1, "z1": 2, "z2": 4, "z3": 6}
GATHER = (
    (2, "z1"),
    (6, "z3"),
    (1, "b"),
    (16, "a"),
    (3, "b"),
    (18, "a"),
    (5, "z2"),
    (17, "a"),
    (22, "a"),
    (4, "z1"),
    (19, "a"),
    (7, "b"),
    (23, "b"),
    (20, "z1"),
    (21, "a"),
)
SCATTER = (
    (23, "z1"),
    (7, "b"),
    (5, "b"),
    (22, "z1"),
    (19, "b"),
    (21, "b"),
    (6, "z1"),
    (3, "b"),
    (20, "a"),
    (18, "a"),
    (17, "b"),
    (4, "z2"),
    (2, "z1"),
    (1, "b"),
    (16, "a"),
)
GATHER_NODES = (0,) + tuple(n for n, _ in GATHER)
SCATTER_NODES = tuple(n for n, _ in SCATTER) + (0,)
GROUP = 4


def swap(node):
    return (node & 6) | (16 if node & 1 else 0) | (1 if node & 16 else 0)


def hop(v, kind):
    pairs = []
    for i in range(32):
        m = 8 if kind == "core" else HOPS[kind]
        pairs.append((i, i ^ (swap(m) if i & 8 and kind != "core" else m)))
    return lax.ppermute(v, ("dp", "fsdp"), pairs)


def near(nodes):
    return [(n, swap(n)) for n in nodes]


def far(nodes):
    return [(8 ^ swap(n), 8 ^ n) for n in nodes]


def local(latents, condition, cotangent, validity, params, moment_one, moment_two):
    outer = lax.axis_size("dp")
    inner = lax.axis_size("fsdp")
    devices = outer * inner
    both = ("dp", "fsdp")
    me = (lax.axis_index("dp") * inner + lax.axis_index("fsdp")).astype(jnp.int32)
    length, _, _, _, rows = shard_geometry(devices)
    shift = ((me * (length % LANES)) % LANES).astype(jnp.int32).reshape(1)
    own = shift_shard(shift, params, rows)
    if (outer, inner) == (4, 8):
        core = jnp.bitwise_and(jnp.right_shift(me, 3), 1)
        own, place = lax.optimization_barrier((own, jnp.stack([me, core])))
        got = {0: own}
        for node, kind in GATHER:
            got[node] = hop(got[node ^ HOPS[kind]], kind)
        pieces = [got[n] for n in GATHER_NODES]
        crossed = []
        for v in pieces:
            crossed.append(hop(v, "core"))
        cuts = [SCATTER_NODES[k : k + GROUP] for k in range(0, len(SCATTER_NODES), GROUP)]
        bo, lg, cg, blocks = run_step(
            devices, place, validity, latents, condition, cotangent, pieces + crossed,
            [[m] for m in near(GATHER_NODES) + far(GATHER_NODES)],
            [near(c) for c in cuts] + [far(c) for c in cuts],
        )
        sums = {}
        for j, cut in enumerate(cuts):
            theirs = hop(blocks[len(cuts) + j], "core")
            for k, node in enumerate(cut):
                sums[node] = (blocks[j][k].astype(F32) + theirs[k].astype(F32)).astype(BF)
        waiting = {n: [] for n in SCATTER_NODES}
        for node, kind in SCATTER:
            half = sums[node]
            if waiting[node]:
                half = half.astype(F32)
                for extra in waiting[node]:
                    half = half + extra.astype(F32)
                half = half.astype(BF)
            waiting[node ^ HOPS[kind]].append(hop(half, kind))
        parts = [sums[0]] + waiting[0]
    else:
        gathered = lax.all_gather(own, both, axis=0, tiled=False)
        every = [[(i, i) for i in range(devices)]]
        bo, lg, cg, (chunks,) = run_step(
            devices, jnp.zeros((2,), jnp.int32), validity, latents, condition, cotangent,
            [gathered], every, every,
        )
        parts = [lax.psum_scatter(chunks, both, scatter_dimension=0, tiled=False)]
    grad, squares = unshift(shift, parts, length)
    if (outer, inner) == (4, 8):
        rounds = ((8,), (16, 1, 17), (2, 4, 6))
    else:
        rounds = tuple((1 << k,) for k in range((devices - 1).bit_length()))
    grad_shard = grad.reshape(-1)[:length]
    for masks in rounds:
        came = [lax.ppermute(squares, both, [(i, i ^ m) for i in range(devices)]) for m in masks]
        for v in came:
            squares = squares + v
    clip_factor = jnp.minimum(1.0, MAX_NORM / (jnp.sqrt(squares[0, 0]) + NORM_EPS))
    clipped = grad_shard * clip_factor
    new_one = BETA_ONE * moment_one + (1.0 - BETA_ONE) * clipped
    new_two = BETA_TWO * moment_two + (1.0 - BETA_TWO) * clipped * clipped
    corrected_one = new_one / (1.0 - BETA_ONE**STEP)
    corrected_two = new_two / (1.0 - BETA_TWO**STEP)
    new_params = params - LEARN_RATE * (
        corrected_one / (jnp.sqrt(corrected_two) + ADAM_EPS) + WEIGHT_DECAY * params
    )
    return (
        bo.reshape(latents.shape), lg.reshape(latents.shape), cg,
        grad_shard, new_params, new_one, new_two,
    )


def solution(mesh):
    both = ("dp", "fsdp")
    in_specs = (
        P(both, None, None), P(both, None), P(both, None, None),
        P(both), P(both), P(both), P(both),
    )
    out_specs = (
        P(both, None, None), P(both, None, None), P(both, None),
        P(both), P(both), P(both), P(both),
    )
    return jax.shard_map(local, mesh=mesh, in_specs=in_specs, out_specs=out_specs, check_vma=False)
```

```python
import functools
import jax
import jax.numpy as jnp
from jax import lax
from jax.experimental import pallas as pl
from jax.experimental.pallas import tpu as pltpu
from jax.sharding import PartitionSpec as P


D = 384
FF = 1536
HEADS = 6
HEAD_DIM = 64
STEP = 3
LANES = 128

NORM_EPS = 1e-06
LEARN_RATE = 0.01
BETA_ONE = 0.9
BETA_TWO = 0.999
ADAM_EPS = 1e-08
WEIGHT_DECAY = 0.1
MAX_NORM = 1.0
GELU_COEF = 0.7978845608028654
CUBIC_COEF = 0.044715

VMEM_LIMIT = 48 * 1024 * 1024


BF = jnp.bfloat16
F32 = jnp.float32

ADA0 = 0
QKV0 = ADA0 + D * 6 * D // LANES
PROJ0 = QKV0 + D * 3 * D // LANES
FIRST0 = PROJ0 + D * D // LANES
SECOND0 = FIRST0 + D * FF // LANES
BIAS0 = SECOND0 + FF * D // LANES
BIAS_LEN = 6 * D + 3 * D + FF + D
TOTAL = BIAS0 * LANES + BIAS_LEN
B_ADA, B_QUERY, B_VALUE, B_PROJ, B_FIRST, B_SECOND = 0, 6 * D, 7 * D, 8 * D, 9 * D, 9 * D + FF

MATRICES = ((ADA0, D, 6 * D), (QKV0, D, 3 * D), (PROJ0, D, D), (FIRST0, D, FF), (SECOND0, FF, D))


def nn(a, b):
    return lax.dot_general(a, b, (((1,), (0,)), ((), ())), preferred_element_type=F32)


def nt(a, b):
    return lax.dot_general(a, b, (((1,), (1,)), ((), ())), preferred_element_type=F32)


def tn(a, b):
    return lax.dot_general(a, b, (((0,), (0,)), ((), ())), preferred_element_type=F32)


def silu(v):
    return v / (1.0 + jnp.exp(-v))


def mean_last(v):
    return jnp.sum(v, axis=-1, keepdims=True) * (1.0 / v.shape[-1])


def shard_geometry(devices):
    length = TOTAL // devices
    starts = [(length * i) // LANES for i in range(devices)]
    shifts = [(length * i) % LANES for i in range(devices)]
    counts = [-(-(shifts[i] + length) // LANES) for i in range(devices)]
    rows = -(-(max(counts) + 1) // 16) * 16
    return length, starts, shifts, counts, rows


def step_kernel(
    devices, seq, batch, slots_in, slots_out,
    me_ref, valid_ref, lat_ref, cond_ref, cot_hbm, *rest,
):
    n_in = len(slots_in)
    pieces = rest[:n_in]
    bo_hbm, lg_hbm, cg_ref = rest[n_in : n_in + 3]
    n_out = len(slots_out)
    outs = rest[n_in + 3 : n_in + 3 + n_out]
    (
        stage, flat, w_ada, w_qkv, w_proj, w_first, w_second, bias,
        normed1, inv1, mixed1, qkv, probs, heads_f, heads_h, projected,
        middle, normed2, inv2, mixed2, slope, gelu_h, mlp_out,
        mod, gmod, gcol, gmlp_h, gpre_h, gmix, cond8, gmod_h,
        cot_ref, bo_ref, lg_ref, sem_cot, sem_bo, sem_lg,
    ) = rest[n_in + 3 + n_out :]
    gmid, gheads, gproj_h, gqkv_h = middle, mlp_out, gmlp_h, gpre_h
    _, starts, shifts, counts, rows = shard_geometry(devices)
    tokens = batch * seq
    scale = HEAD_DIM ** (-0.5)
    me = me_ref[0]
    core_one = me_ref[1] == 1

    def owner(masks):
        return jnp.bitwise_xor(me, jnp.where(core_one, masks[1], masks[0]))

    copy_cot = pltpu.make_async_copy(cot_hbm, cot_ref, sem_cot)
    copy_bo = pltpu.make_async_copy(bo_ref, bo_hbm, sem_bo)
    copy_lg = pltpu.make_async_copy(lg_ref, lg_hbm, sem_lg)
    copy_cot.start()
    for ref, slots in zip(pieces, slots_in):
        for j, masks in enumerate(slots):
            stage[owner(masks)] = ref[...] if len(slots) == 1 else ref[j]

    chunk = 256

    def norm_one(i, carry):
        rs = pl.ds(pl.multiple_of(i * chunk, chunk), chunk)
        v = lat_ref[rs, :]
        cen = v - mean_last(v)
        inv = lax.rsqrt(mean_last(cen * cen) + NORM_EPS)
        normed1[rs, :] = cen * inv
        inv1[rs, :] = jnp.broadcast_to(inv, (chunk, LANES))
        return carry

    lax.fori_loop(0, tokens // chunk, norm_one, 0)

    for i in range(devices):
        g = starts[i]
        n = counts[i]
        block = stage[i].astype(F32)
        if shifts[i] == 0:
            flat[g : g + n, :] = block[:n]
        else:
            flat[g : g + 1, :] = flat[g : g + 1, :] + block[:1]
            flat[g + 1 : g + n, :] = block[1:n]

    for w, (base, height, width) in zip((w_ada, w_qkv, w_proj, w_first, w_second), MATRICES):
        tiles = width // LANES
        for c in range(tiles):
            w[:, c * LANES : (c + 1) * LANES] = flat[pl.ds(base + c, height, stride=tiles), :].astype(BF)
    for r in range(BIAS_LEN // LANES):
        bias[:, r * LANES : (r + 1) * LANES] = flat[BIAS0 + r : BIAS0 + r + 1, :]

    cond8[...] = jnp.zeros_like(cond8)
    cond8[0:batch, :] = silu(cond_ref[...])
    ch = cond8[...].astype(BF)
    mod[...] = nn(ch, w_ada[...]) + bias[:, B_ADA : B_ADA + 6 * D]

    def part(ref, b, k):
        return ref[pl.ds(b, 1), k * D : (k + 1) * D]

    def mix_one(i, carry):
        b = i // (seq // chunk)
        rs = pl.ds(pl.multiple_of(i * chunk, chunk), chunk)
        mixed1[rs, :] = (normed1[rs, :] * (1.0 + part(mod, b, 1)) + part(mod, b, 0)).astype(BF)
        return carry

    lax.fori_loop(0, tokens // chunk, mix_one, 0)

    for j in range(3):
        cols = slice(j * D, (j + 1) * D)
        acc = nn(mixed1[...], w_qkv[:, cols])
        if j == 0:
            acc = acc + bias[:, B_QUERY : B_QUERY + D]
        if j == 2:
            acc = acc + bias[:, B_VALUE : B_VALUE + D]
        qkv[:, cols] = acc.astype(BF)

    lane = lax.broadcasted_iota(jnp.int32, (1, LANES), 1)
    low = lane < HEAD_DIM
    zero_bf = jnp.zeros((), BF)

    def keep(v, half):
        return jnp.where(low if half == 0 else jnp.logical_not(low), v, zero_bf)

    pairs = HEADS // 2

    def attn(b, carry):
        rs = pl.ds(pl.multiple_of(b * seq, seq), seq)
        for h in range(pairs):
            q = qkv[rs, h * LANES : (h + 1) * LANES]
            k = qkv[rs, D + h * LANES : D + (h + 1) * LANES]
            v = qkv[rs, 2 * D + h * LANES : 2 * D + (h + 1) * LANES]
            res = []
            for half in range(2):
                s = nt(keep(q, half), k) * scale
                e = jnp.exp(s - jnp.max(s, axis=-1, keepdims=True))
                p = e * (1.0 / jnp.sum(e, axis=-1, keepdims=True))
                probs[b * HEADS + 2 * h + half] = p
                res.append(nn(p.astype(BF), v))
            o = jnp.where(low, res[0], res[1])
            heads_f[rs, h * LANES : (h + 1) * LANES] = o
            heads_h[rs, h * LANES : (h + 1) * LANES] = o.astype(BF)
        return carry

    lax.fori_loop(0, batch, attn, 0)

    projected[...] = nn(heads_h[...], w_proj[...]) + bias[:, B_PROJ : B_PROJ + D]

    def mid(i, carry):
        b = i // (seq // chunk)
        rs = pl.ds(pl.multiple_of(i * chunk, chunk), chunk)
        m = lat_ref[rs, :] + part(mod, b, 2) * projected[rs, :]
        middle[rs, :] = m
        cen = m - mean_last(m)
        inv = lax.rsqrt(mean_last(cen * cen) + NORM_EPS)
        n2 = cen * inv
        normed2[rs, :] = n2
        inv2[rs, :] = jnp.broadcast_to(inv, (chunk, LANES))
        mixed2[rs, :] = (n2 * (1.0 + part(mod, b, 4)) + part(mod, b, 3)).astype(BF)
        return carry

    lax.fori_loop(0, tokens // chunk, mid, 0)

    fchunk = 256
    for j in range(FF // fchunk):
        cols = slice(j * fchunk, (j + 1) * fchunk)
        u = nn(mixed2[...], w_first[:, cols]) + bias[:, B_FIRST + j * fchunk : B_FIRST + (j + 1) * fchunk]
        uu = u * u
        t = jnp.tanh(GELU_COEF * (u + CUBIC_COEF * uu * u))
        half_u = 0.5 * u
        gelu_h[:, cols] = (half_u * (1.0 + t)).astype(BF)
        slope[:, cols] = 0.5 * (1.0 + t) + half_u * (1.0 - t * t) * GELU_COEF * (
            1.0 + 3.0 * CUBIC_COEF * uu
        )
    mlp_out[...] = nn(gelu_h[...], w_second[...]) + bias[:, B_SECOND : B_SECOND + D]

    gcol[...] = jnp.zeros_like(gcol)
    gmod[...] = jnp.zeros_like(gmod)

    def add_col(ref, b, k, v):
        ref[pl.ds(b, 1), k * D : (k + 1) * D] += jnp.sum(v, axis=0, keepdims=True)

    def out_step(i, carry):
        b = i // (seq // chunk)
        rs = pl.ds(pl.multiple_of(i * chunk, chunk), chunk)
        mo = mlp_out[rs, :]
        gate = part(mod, b, 5)
        bo_ref[rs, :] = middle[rs, :] + gate * mo
        up = cot_ref[rs, :] * valid_ref[b].astype(F32)
        add_col(gmod, b, 5, up * mo)
        gm = up * gate
        gcol[:, B_SECOND : B_SECOND + D] += jnp.sum(gm, axis=0, keepdims=True)
        gmlp_h[rs, :] = gm.astype(BF)
        return carry

    copy_cot.wait()
    lax.fori_loop(0, tokens // chunk, out_step, 0)
    copy_bo.start()

    def put(base, tiles, height, row0, c0, value):
        for c in range(value.shape[1] // LANES):
            flat[pl.ds(base + row0 * tiles + c0 + c, height, stride=tiles), :] = value[
                :, c * LANES : (c + 1) * LANES
            ]

    for j in range(FF // D):
        rr = slice(j * D, (j + 1) * D)
        put(SECOND0, D // LANES, D, j * D, 0, tn(gelu_h[:, rr], gmlp_h[...]))
    for j in range(FF // fchunk):
        cols = slice(j * fchunk, (j + 1) * fchunk)
        gp = nt(gmlp_h[...], w_second[cols, :]) * slope[:, cols]
        gcol[:, B_FIRST + j * fchunk : B_FIRST + (j + 1) * fchunk] = jnp.sum(gp, axis=0, keepdims=True)
        gpre_h[:, cols] = gp.astype(BF)
    for j in range(FF // D):
        cols = slice(j * D, (j + 1) * D)
        put(FIRST0, FF // LANES, D, 0, j * (D // LANES), tn(mixed2[...], gpre_h[:, cols]))
    gmix[...] = nt(gpre_h[...], w_first[...])

    def back_two(i, carry):
        b = i // (seq // chunk)
        rs = pl.ds(pl.multiple_of(i * chunk, chunk), chunk)
        g = gmix[rs, :]
        n2 = normed2[rs, :]
        add_col(gmod, b, 3, g)
        add_col(gmod, b, 4, g * n2)
        e = g * (1.0 + part(mod, b, 4))
        up = cot_ref[rs, :] * valid_ref[b].astype(F32)
        inv = inv2[rs, 0:1]
        gm = up + inv * (e - mean_last(e) - n2 * mean_last(e * n2))
        gmid[rs, :] = gm
        add_col(gmod, b, 2, gm * projected[rs, :])
        gp = gm * part(mod, b, 2)
        gcol[:, B_PROJ : B_PROJ + D] += jnp.sum(gp, axis=0, keepdims=True)
        gproj_h[rs, :] = gp.astype(BF)
        return carry

    lax.fori_loop(0, tokens // chunk, back_two, 0)

    put(PROJ0, D // LANES, D, 0, 0, tn(heads_h[...], gproj_h[...]))
    gheads[...] = nt(gproj_h[...], w_proj[...])

    def attn_back(b, carry):
        rs = pl.ds(pl.multiple_of(b * seq, seq), seq)
        for h in range(pairs):
            ls = slice(h * LANES, (h + 1) * LANES)
            q = qkv[rs, h * LANES : (h + 1) * LANES]
            k = qkv[rs, D + h * LANES : D + (h + 1) * LANES]
            v = qkv[rs, 2 * D + h * LANES : 2 * D + (h + 1) * LANES]
            gh = gheads[rs, ls]
            prod = gh * heads_f[rs, ls]
            ghh = gh.astype(BF)
            dq, dk, dv = [], [], []
            for half in range(2):
                delta = jnp.sum(
                    jnp.where(low if half == 0 else jnp.logical_not(low), prod, 0.0),
                    axis=-1, keepdims=True,
                )
                p = probs[b * HEADS + 2 * h + half]
                gp = nt(keep(ghh, half), v)
                gs = (p * (gp - delta)).astype(BF)
                dq.append(nn(gs, k))
                dk.append(tn(gs, q))
                dv.append(tn(p.astype(BF), ghh))
            gq = jnp.where(low, dq[0], dq[1]) * scale
            gk = jnp.where(low, dk[0], dk[1]) * scale
            gv = jnp.where(low, dv[0], dv[1])
            gcol[:, B_QUERY + h * LANES : B_QUERY + (h + 1) * LANES] += jnp.sum(gq, axis=0, keepdims=True)
            gcol[:, B_VALUE + h * LANES : B_VALUE + (h + 1) * LANES] += jnp.sum(gv, axis=0, keepdims=True)
            gqkv_h[rs, h * LANES : (h + 1) * LANES] = gq.astype(BF)
            gqkv_h[rs, D + h * LANES : D + (h + 1) * LANES] = gk.astype(BF)
            gqkv_h[rs, 2 * D + h * LANES : 2 * D + (h + 1) * LANES] = gv.astype(BF)
        return carry

    lax.fori_loop(0, batch, attn_back, 0)

    for j in range(3):
        cols = slice(j * D, (j + 1) * D)
        put(QKV0, 3 * D // LANES, D, 0, j * (D // LANES), tn(mixed1[...], gqkv_h[:, cols]))
    gmix[...] = nt(gqkv_h[:, : 3 * D], w_qkv[...])

    def back_one(i, carry):
        b = i // (seq // chunk)
        rs = pl.ds(pl.multiple_of(i * chunk, chunk), chunk)
        g = gmix[rs, :]
        n1 = normed1[rs, :]
        add_col(gmod, b, 0, g)
        add_col(gmod, b, 1, g * n1)
        e = g * (1.0 + part(mod, b, 1))
        inv = inv1[rs, 0:1]
        lg_ref[rs, :] = gmid[rs, :] + inv * (e - mean_last(e) - n1 * mean_last(e * n1))
        return carry

    lax.fori_loop(0, tokens // chunk, back_one, 0)
    copy_lg.start()

    gmod_h[...] = gmod[...].astype(BF)
    for j in range(6):
        cols = slice(j * D, (j + 1) * D)
        put(ADA0, 6 * D // LANES, D, 0, j * (D // LANES), tn(ch, gmod_h[:, cols]))
    gcol[:, B_ADA : B_ADA + 6 * D] = jnp.sum(gmod[...], axis=0, keepdims=True)
    cg = nt(gmod_h[...], w_ada[...])[0:batch]
    cv = cond_ref[...]
    sig = 1.0 / (1.0 + jnp.exp(-cv))
    cg_ref[...] = cg * (sig * (1.0 + cv * (1.0 - sig)))

    for r in range(BIAS_LEN // LANES):
        flat[BIAS0 + r : BIAS0 + r + 1, :] = gcol[:, r * LANES : (r + 1) * LANES]

    for i in range(devices):
        g = starts[i]
        stage[i] = flat[g : g + rows, :].astype(BF)
    for ref, slots in zip(outs, slots_out):
        for j, masks in enumerate(slots):
            ref[j] = stage[owner(masks)]
    copy_bo.wait()
    copy_lg.wait()


def run_step(
    devices, place, validity, latents, condition, cotangent, pieces, slots_in, slots_out
):
    batch, seq, _ = latents.shape
    tokens = batch * seq
    _, starts, _, _, rows = shard_geometry(devices)
    flat_rows = -(-(starts[-1] + rows) // 16) * 16
    vm = pl.BlockSpec(memory_space=pltpu.VMEM)
    hb = pl.BlockSpec(memory_space=pl.ANY)
    sm = pl.BlockSpec(memory_space=pltpu.SMEM)
    out_shape = [
        jax.ShapeDtypeStruct((tokens, D), F32),
        jax.ShapeDtypeStruct((tokens, D), F32),
        jax.ShapeDtypeStruct((batch, D), F32),
    ] + [
        pltpu.VMEM((len(slots), rows, LANES), BF) for slots in slots_out
    ]
    V = pltpu.VMEM
    scratch = [
        V((devices, rows, LANES), BF),
        V((flat_rows, LANES), F32),
        V((D, 6 * D), BF), V((D, 3 * D), BF), V((D, D), BF), V((D, FF), BF), V((FF, D), BF),
        V((1, BIAS_LEN), F32),
        V((tokens, D), F32), V((tokens, LANES), F32), V((tokens, D), BF), V((tokens, 3 * D), BF),
        V((batch * HEADS, seq, seq), F32), V((tokens, D), F32), V((tokens, D), BF), V((tokens, D), F32),
        V((tokens, D), F32), V((tokens, D), F32), V((tokens, LANES), F32), V((tokens, D), BF),
        V((tokens, FF), F32), V((tokens, FF), BF), V((tokens, D), F32),
        V((8, 6 * D), F32), V((8, 6 * D), F32), V((1, BIAS_LEN), F32),
        V((tokens, D), BF), V((tokens, FF), BF), V((tokens, D), F32), V((8, D), F32), V((8, 6 * D), BF),
        V((tokens, D), F32), V((tokens, D), F32), V((tokens, D), F32),
        pltpu.SemaphoreType.DMA, pltpu.SemaphoreType.DMA, pltpu.SemaphoreType.DMA,
    ]
    body = functools.partial(step_kernel, devices, seq, batch, slots_in, slots_out)
    res = pl.pallas_call(
        body,
        out_shape=out_shape,
        in_specs=[sm, sm, vm, vm, hb] + [vm] * len(pieces),
        out_specs=[hb, hb, vm] + [vm] * len(slots_out),
        scratch_shapes=scratch,
        compiler_params=pltpu.CompilerParams(vmem_limit_bytes=VMEM_LIMIT),
        name="step",
    )(
        place, validity,
        pltpu.with_memory_space_constraint(latents.reshape(tokens, D), pltpu.VMEM),
        condition, cotangent.reshape(tokens, D),
        *[pltpu.with_memory_space_constraint(p, pltpu.VMEM) for p in pieces],
    )
    return res[0], res[1], res[2], res[3:]


def shift_kernel(s_ref, x_ref, o_ref):
    s = s_ref[0]
    rolled = pltpu.roll(x_ref[...], s, 1)
    above = pltpu.roll(rolled, 1, 0)
    lane = lax.broadcasted_iota(jnp.int32, rolled.shape, 1)
    o_ref[...] = jnp.where(lane < s, above, rolled).astype(BF)


def shift_shard(shift, params, rows):
    padded = jnp.pad(params, (0, rows * LANES - params.shape[0])).reshape(rows, LANES)
    return pl.pallas_call(
        shift_kernel,
        out_shape=pltpu.VMEM((rows, LANES), BF),
        in_specs=[pl.BlockSpec(memory_space=pltpu.SMEM), pl.BlockSpec(memory_space=pltpu.VMEM)],
        out_specs=pl.BlockSpec(memory_space=pltpu.VMEM),
        name="shift",
    )(shift, pltpu.with_memory_space_constraint(padded, pltpu.VMEM))


def unshift_kernel(length, n, s_ref, *refs):
    s = s_ref[0]
    total = refs[0][...].astype(F32)
    for r in refs[1:n]:
        total = total + r[...].astype(F32)
    g_ref, sq_ref = refs[n:]
    rows = total.shape[0]
    back = jnp.where(s == 0, 0, LANES - s)
    rolled = pltpu.roll(total, back, 1)
    below = pltpu.roll(rolled, rows - 1, 0)
    lane = lax.broadcasted_iota(jnp.int32, rolled.shape, 1)
    row = lax.broadcasted_iota(jnp.int32, rolled.shape, 0)
    out = jnp.where(lane < LANES - s, rolled, below)
    out = jnp.where(row * LANES + lane < length, out, 0.0)
    g_ref[...] = out
    sq_ref[...] = jnp.full(sq_ref.shape, jnp.sum(out * out), F32)


def unshift(shift, parts, length):
    rows = parts[0].shape[0]
    return pl.pallas_call(
        functools.partial(unshift_kernel, length, len(parts)),
        out_shape=[pltpu.VMEM((rows, LANES), F32), pltpu.VMEM((8, LANES), F32)],
        in_specs=[pl.BlockSpec(memory_space=pltpu.SMEM)]
        + [pl.BlockSpec(memory_space=pltpu.VMEM)] * len(parts),
        out_specs=[pl.BlockSpec(memory_space=pltpu.VMEM)] * 2,
        name="unshift",
    )(shift, *[pltpu.with_memory_space_constraint(p, pltpu.VMEM) for p in parts])


HOPS = {"a": 16, "b": 1, "z1": 2, "z2": 4, "z3": 6}
GATHER = (
    (4, "z2"),
    (1, "b"),
    (16, "a"),
    (2, "z1"),
    (17, "a"),
    (3, "z1"),
    (20, "a"),
    (5, "b"),
    (6, "z1"),
    (18, "a"),
    (21, "b"),
    (19, "z1"),
    (7, "b"),
    (22, "a"),
    (23, "z1"),
)
SCATTER = (
    (23, "b"),
    (7, "z1"),
    (21, "b"),
    (22, "a"),
    (19, "z1"),
    (5, "b"),
    (6, "z1"),
    (3, "b"),
    (20, "a"),
    (18, "z1"),
    (17, "b"),
    (4, "z2"),
    (16, "a"),
    (2, "z1"),
    (1, "b"),
)
GATHER_NODES = (0,) + tuple(n for n, _ in GATHER)
SCATTER_NODES = tuple(n for n, _ in SCATTER) + (0,)
GROUP = 4


def swap(node):
    return (node & 6) | (16 if node & 1 else 0) | (1 if node & 16 else 0)


def hop(v, kind):
    pairs = []
    for i in range(32):
        m = 8 if kind == "core" else HOPS[kind]
        pairs.append((i, i ^ (swap(m) if i & 8 and kind != "core" else m)))
    return lax.ppermute(v, ("dp", "fsdp"), pairs)


def near(nodes):
    return [(n, swap(n)) for n in nodes]


def far(nodes):
    return [(8 ^ swap(n), 8 ^ n) for n in nodes]


def local(latents, condition, cotangent, validity, params, moment_one, moment_two):
    outer = lax.axis_size("dp")
    inner = lax.axis_size("fsdp")
    devices = outer * inner
    both = ("dp", "fsdp")
    me = (lax.axis_index("dp") * inner + lax.axis_index("fsdp")).astype(jnp.int32)
    length, _, _, _, rows = shard_geometry(devices)
    shift = ((me * (length % LANES)) % LANES).astype(jnp.int32).reshape(1)
    own = shift_shard(shift, params, rows)
    if (outer, inner) == (4, 8):
        core = jnp.bitwise_and(jnp.right_shift(me, 3), 1)
        own, place = lax.optimization_barrier((own, jnp.stack([me, core])))
        got = {0: own}
        for node, kind in GATHER:
            got[node] = hop(got[node ^ HOPS[kind]], kind)
        pieces = [got[n] for n in GATHER_NODES]
        crossed = []
        for v in pieces:
            crossed.append(hop(v, "core"))
        cuts = [SCATTER_NODES[k : k + GROUP] for k in range(0, len(SCATTER_NODES), GROUP)]
        bo, lg, cg, blocks = run_step(
            devices, place, validity, latents, condition, cotangent, pieces + crossed,
            [[m] for m in near(GATHER_NODES) + far(GATHER_NODES)],
            [near(c) for c in cuts] + [far(c) for c in cuts],
        )
        sums = {}
        for j, cut in enumerate(cuts):
            theirs = hop(blocks[len(cuts) + j], "core")
            for k, node in enumerate(cut):
                sums[node] = (blocks[j][k].astype(F32) + theirs[k].astype(F32)).astype(BF)
        waiting = {n: [] for n in SCATTER_NODES}
        for node, kind in SCATTER:
            half = sums[node]
            if waiting[node]:
                half = half.astype(F32)
                for extra in waiting[node]:
                    half = half + extra.astype(F32)
                half = half.astype(BF)
            waiting[node ^ HOPS[kind]].append(hop(half, kind))
        parts = [sums[0]] + waiting[0]
    else:
        gathered = lax.all_gather(own, both, axis=0, tiled=False)
        every = [[(i, i) for i in range(devices)]]
        bo, lg, cg, (chunks,) = run_step(
            devices, jnp.zeros((2,), jnp.int32), validity, latents, condition, cotangent,
            [gathered], every, every,
        )
        parts = [lax.psum_scatter(chunks, both, scatter_dimension=0, tiled=False)]
    grad, squares = unshift(shift, parts, length)
    if (outer, inner) == (4, 8):
        rounds = ((8,), (16, 1, 17), (2, 4, 6))
    else:
        rounds = tuple((1 << k,) for k in range((devices - 1).bit_length()))
    grad_shard = grad.reshape(-1)[:length]
    for k, masks in enumerate(rounds):
        came = [lax.ppermute(squares, both, [(i, i ^ m) for i in range(devices)]) for m in masks]
        for v in came:
            squares = squares + v
        if k == 0:
            squares, grad_shard = lax.optimization_barrier((squares, grad_shard))
    clip_factor = jnp.minimum(1.0, MAX_NORM / (jnp.sqrt(squares[0, 0]) + NORM_EPS))
    clipped = grad_shard * clip_factor
    new_one = BETA_ONE * moment_one + (1.0 - BETA_ONE) * clipped
    new_two = BETA_TWO * moment_two + (1.0 - BETA_TWO) * clipped * clipped
    corrected_one = new_one / (1.0 - BETA_ONE**STEP)
    corrected_two = new_two / (1.0 - BETA_TWO**STEP)
    new_params = params - LEARN_RATE * (
        corrected_one / (jnp.sqrt(corrected_two) + ADAM_EPS) + WEIGHT_DECAY * params
    )
    return (
        bo.reshape(latents.shape), lg.reshape(latents.shape), cg,
        grad_shard, new_params, new_one, new_two,
    )


def solution(mesh):
    both = ("dp", "fsdp")
    in_specs = (
        P(both, None, None), P(both, None), P(both, None, None),
        P(both), P(both), P(both), P(both),
    )
    out_specs = (
        P(both, None, None), P(both, None, None), P(both, None),
        P(both), P(both), P(both), P(both),
    )
    return jax.shard_map(local, mesh=mesh, in_specs=in_specs, out_specs=out_specs, check_vma=False)
```
